32 devices in a mesh: rep: 2 (over y), blk: 4 (over z), sect: 2 (over x), sub: 2 (over core).
Axes of the slice: x: 2, y: 2, z: 4, core: 2. Of those that a mesh axis runs over, the one named last changes fastest.
Arguments:
- query_latent: bfloat16 [64, 128, 512], P(('rep', 'blk')), parts along dimension 0, may hold values from -192 to 192
- query_rope: bfloat16 [64, 64, 128], P(('rep', 'blk')), parts along dimension 0, may hold values from -18 to 18
- cache_latent: bfloat16 [32, 256, 512], P(('rep', 'blk', 'sect', 'sub')), parts along dimension 0, may hold values from -16 to 16
- cache_rope: bfloat16 [32, 64, 256], P(('rep', 'blk', 'sect', 'sub')), parts along dimension 0, may hold values from -4.5 to 4.5
- lengths: int32 [32], P('rep'), parts along dimension 0, may hold values from 64 to 256, as said below
- positions: int32 [64], P(('rep', 'blk')), parts along dimension 0, may hold values from 2048 to 4095
- value_weight: bfloat16 [128, 512, 128], P(('sect', 'sub')), may hold values from -0.25 to 0.25
Outputs:
- attended: bfloat16 [64, 128, 128], P(('rep', 'blk'), ('sect', 'sub')), parts along dimension 0
The draws below stay inside these ranges and needn't reach their ends.
There are 2 independent parts, one for each index of `rep`. The reference program is written for one: setup_inputs(seed, part) draws one part's arguments, and reference() takes and returns one part's arrays. A program takes and returns all parts, laid end to end along the dimension named above; an argument that names none is the same for every part. Nothing has to cross between parts.
Inputs may be any that keep to these rules, and one draw needn't show every extreme that they name: `lengths`: in every draw some block has all 256 slots valid.
All inputs are finite; a program needn't handle non-finite values.
Results may differ from the reference program's by a relative error of at most 0.0075.
Values may be sent and summed in bfloat16 or wider, within the bound.
A program may use at most 64 MiB of HBM per device.

```python
import math
import jax
import jax.numpy as jnp
from jax import lax

L = 512
R = 64
H = 128
DV = 128
T_DEV = 256
QUERIES = 32
BLOCKS = 16
CACHE = 4096


def joint_draw(key):
    cache_values = jnp.clip(jax.random.normal(jax.random.fold_in(key, 1), (BLOCKS, T_DEV, L), jnp.float32), -4.5, 4.5)
    query_values = jnp.clip(3.0 * jax.random.normal(jax.random.fold_in(key, 2), (QUERIES, H, L), jnp.float32), -18.0, 18.0)
    return (query_values, cache_values)


def draw_query_latent(key, part):
    return joint_draw(key)[0].astype(jnp.bfloat16)


def draw_cache_latent(key, part):
    return joint_draw(key)[1].astype(jnp.bfloat16)


def draw_query_rope(key, part):
    values = jnp.clip(3.0 * jax.random.normal(jax.random.fold_in(key, 8), (QUERIES, R, H), jnp.float32), -18.0, 18.0)
    return values.astype(jnp.bfloat16)


def draw_lengths(key, part):
    counts = jax.random.randint(jax.random.fold_in(key, 21), (BLOCKS,), T_DEV // 4, T_DEV + 1)
    fullest = jax.random.randint(jax.random.fold_in(key, 22), (), 0, BLOCKS)
    return jnp.where(jnp.arange(BLOCKS) == fullest, T_DEV, counts).astype(jnp.int32)


def touch_ends(result, own_key, least, high):
    index_at = [jax.random.randint(jax.random.fold_in(own_key, axis), (), 0, length) for axis, length in enumerate(result.shape)]
    longest = result.shape.index(max(result.shape))
    neighbour = index_at[:longest] + [(index_at[longest] + 1) % result.shape[longest]] + index_at[longest + 1:]
    return result.at[tuple(index_at)].set(least).at[tuple(neighbour)].set(high)


def block_scale(own_key, dims, split, low, high):
    loudness, own = 1.0, jax.random.fold_in(own_key, 6)
    for axis_at, shards_of in split:
        draws = jnp.exp(jax.random.uniform(jax.random.fold_in(own, axis_at), (shards_of,), jnp.float32, low / len(split), high / len(split)))
        loudness = loudness * jnp.repeat(draws, dims[axis_at] // shards_of).reshape([-1 if axis == axis_at else 1 for axis in range(len(dims))])
    return loudness


def bell_draw(own_key, extent, scale, limit, cuts=(), held_as=jnp.bfloat16):
    values = jax.random.normal(own_key, extent, jnp.float32) * scale
    if len(cuts) > 0:
        values = block_scale(own_key, extent, cuts, -0.22, 0.18) * values
    return jnp.clip(values, min=-limit, max=limit).astype(held_as)


def setup_inputs(seed: int = 0, part: int = 0) -> dict:
    seeds = jax.random.split(jax.random.key(seed), 8)
    own_keys = jax.random.split(jax.random.fold_in(seeds[7], part), 8)
    return {
        "query_latent": draw_query_latent(jax.random.fold_in(jax.random.fold_in(seeds[7], part), 71), part),
        "query_rope": draw_query_rope(jax.random.fold_in(jax.random.fold_in(seeds[7], part), 71), part),
        "cache_latent": draw_cache_latent(jax.random.fold_in(jax.random.fold_in(seeds[7], part), 71), part),
        "cache_rope": bell_draw(own_keys[3], (BLOCKS, R, T_DEV), 1.0, 4.5, ((0, 16),)),
        "lengths": draw_lengths(jax.random.fold_in(jax.random.fold_in(seeds[7], part), 71), part),
        "positions": touch_ends(jax.random.randint(own_keys[5], (QUERIES,), CACHE // 2, CACHE), jax.random.fold_in(own_keys[5], 1), CACHE // 2, CACHE - 1).astype(jnp.int32),
        "value_weight": bell_draw(seeds[6], (H, L, DV), L ** -0.5, 0.25, ((0, 4),)),
    }


lowest_score = -1e+30

def reference(query_latent, query_rope, cache_latent, cache_rope, lengths, positions, value_weight):
    score_scale = 1.0 / math.sqrt(L + R)
    flat_latent = cache_latent.reshape(CACHE, L)
    flat_rope = jnp.transpose(cache_rope, (1, 0, 2)).reshape(R, CACHE)
    places = jnp.arange(CACHE, dtype=jnp.int32)
    block_fill = jnp.repeat(lengths, T_DEV, total_repeat_length=CACHE)
    filled = places % T_DEV < block_fill
    wide_weight = value_weight.astype(jnp.float32)

    def one_query(inputs):
        latent_row, rope_row, position = inputs
        scores = lax.dot_general(latent_row, flat_latent, (((1,), (1,)), ((), ())), preferred_element_type=jnp.float32)
        scores = scores + jnp.dot(rope_row.T, flat_rope, preferred_element_type=jnp.float32)
        scores = scores * score_scale
        visible = (filled & (places <= position))[None, :]
        scores = jnp.where(visible, scores, lowest_score)
        top = lax.optimization_barrier(jnp.max(scores, axis=1, keepdims=True))
        weights = jnp.where(visible, jnp.exp(scores - top), 0.0)
        total = lax.optimization_barrier(jnp.sum(weights, axis=1, keepdims=True))
        mixed = jnp.dot(weights.astype(jnp.bfloat16), flat_latent, preferred_element_type=jnp.float32)
        latent = (mixed / total).astype(jnp.bfloat16)
        return jnp.einsum('hl,hld->hd', latent.astype(jnp.float32), wide_weight).astype(jnp.bfloat16)
    return lax.map(one_query, (query_latent, query_rope, positions))
```

```python
import functools
import math

import jax
import jax.numpy as jnp
from jax import lax
from jax.experimental import pallas as pl
from jax.experimental.pallas import tpu as pltpu
from jax.sharding import PartitionSpec as P

lowest_score = -1e30
first_top = -1e29
LANES = 128
MESH = pl.DeviceIdType.MESH


def spread(column, width):
    return jnp.concatenate([column] * (width // LANES), axis=1)


def kernel(
    sizes, query_hbm, rope_q_hbm, latent_hbm, rope_hbm, length_hbm, position_hbm, weight_hbm,
    out_ref,
    rope_q_ref, length_ref, position_ref, query_buf, rope_q_buf, latent_buf, rope_buf, weight_buf, place_buf,
    top_buf, sum_buf, acc_buf,
    local_sem, z_send, z_recv, x_send, x_recv, pair_send, pair_recv, side_send, side_recv,
):
    blk_count, sect_count, sub_count, cuts, chunk_heads = sizes
    query_count, own_heads, latent_width = query_buf.shape
    rope_width = rope_q_hbm.shape[1]
    token_count = latent_hbm.shape[1]
    cut = token_count // cuts
    unit = sub_count * cut
    rows = query_count * own_heads
    chunk_count = own_heads // chunk_heads
    chunk_rows = query_count * chunk_heads
    score_scale = math.log2(math.e) / math.sqrt(latent_width + rope_width)
    side = tuple(h for h in range(cuts) if h >= cuts // 2) if sect_count == 2 and cuts > 1 else ()
    z = lax.axis_index("blk")
    x = lax.axis_index("sect")
    s = lax.axis_index("sub")
    last_z = blk_count - 1
    other = lax.rem(x + 1, sect_count)

    barrier = pltpu.get_barrier_semaphore()

    def greet(device_id):
        pl.semaphore_signal(barrier, inc=1, device_id=device_id, device_id_type=MESH)

    for step in range(1, sub_count):
        greet({"sub": lax.rem(s + step, sub_count)})
    for step in range(1, sect_count):
        greet({"sect": lax.rem(x + step, sect_count)})

    @pl.when(z > 0)
    def _():
        greet({"blk": z - 1})

    @pl.when(z < last_z)
    def _():
        greet({"blk": z + 1})

    heads_at = pl.multiple_of((x * sub_count + s) * own_heads, own_heads)
    small_copies = [
        pltpu.make_async_copy(source, landing, local_sem.at[i])
        for i, (source, landing) in enumerate((
            (rope_q_hbm, rope_q_ref), (length_hbm, length_ref), (position_hbm, position_ref),
            (query_hbm.at[:, pl.ds(heads_at, own_heads), :], query_buf),
        ))
    ]
    weight_copy = pltpu.make_async_copy(weight_hbm, weight_buf, local_sem.at[4])

    def held(j, xx, ss, h):
        return latent_buf.at[j, xx, ss, pl.ds(h * cut, cut)], rope_buf.at[j, xx, h, ss]

    def own(h):
        return latent_hbm.at[0, pl.ds(h * cut, cut)], rope_hbm.at[0, :, pl.ds(h * cut, cut)]

    own_copies = [
        pltpu.make_async_copy(source, landing, local_sem.at[5 + 2 * h + i])
        for h in range(cuts)
        for i, (source, landing) in enumerate(zip(own(h), held(z, x, s, h)))
    ]

    class Send:
        def __init__(self, source, landing, send_sem, recv_sem, device_id):
            self.copies = [
                pltpu.make_async_remote_copy(
                    src_ref=source[i], dst_ref=landing[i], send_sem=send_sem.at[i], recv_sem=recv_sem.at[i],
                    device_id=device_id, device_id_type=MESH,
                )
                for i in range(2)
            ]

        def start(self):
            for copy in self.copies:
                copy.start()

        def wait_recv(self):
            for copy in self.copies:
                copy.wait_recv()

        def wait_send(self):
            for copy in self.copies:
                copy.wait_send()

    def z_copy(source, j, h, way, target):
        return Send(source, held(j, x, s, h), z_send.at[way, j, h], z_recv.at[j, h], {"blk": target})

    def x_copy(source, j, h, step):
        return Send(
            source, held(j, x, s, h), x_send.at[step - 1, j, h], x_recv.at[step - 1, j, h],
            {"sect": lax.rem(x + step, sect_count)},
        )

    def x_arrival(j, h, step):
        here = held(j, source_section(step), s, h)
        return Send(here, here, x_send.at[step - 1, j, h], x_recv.at[step - 1, j, h], {"sect": x})

    def pair_copy(source, j, xx, h, step):
        return Send(
            source, held(j, xx, s, h), pair_send.at[step - 1, j, xx, h], pair_recv.at[step - 1, j, xx, h],
            {"sub": lax.rem(s + step, sub_count)},
        )

    def pair_arrival(j, xx, h, step):
        here = held(j, xx, lax.rem(s + sub_count - step, sub_count), h)
        return Send(here, here, pair_send.at[step - 1, j, xx, h], pair_recv.at[step - 1, j, xx, h], {"sub": s})

    def side_copy(j, h, way, target):
        place = held(j, other, s, h)
        return Send(place, place, side_send.at[way, h], side_recv.at[way, h], {"blk": target})

    def source_section(step):
        return lax.rem(x + sect_count - step, sect_count)

    def to_pair(source, j, xx, h):
        for step in range(1, sub_count):
            pair_copy(source, j, xx, h, step).start()

    for copy in small_copies + own_copies:
        copy.start()
    neighbours = jnp.where(z > 0, 1, 0) + jnp.where(z < last_z, 1, 0)
    pl.semaphore_wait(barrier, sub_count - 1 + sect_count - 1 + neighbours)

    for h in range(cuts):
        @pl.when(z < last_z)
        def _():
            z_copy(own(h), z, h, 0, z + 1).start()

        @pl.when(z > 0)
        def _():
            z_copy(own(h), z, h, 1, z - 1).start()

        for step in range(1, sect_count):
            x_copy(own(h), z, h, step).start()
        to_pair(own(h), z, x, h)
    weight_copy.start()

    for copy in small_copies:
        copy.wait()
    for q in range(query_count):
        turned = jnp.transpose(rope_q_ref[q].astype(jnp.float32)).astype(jnp.bfloat16)
        rope_q_buf[q] = turned
        place_buf[pl.ds(q * own_heads, own_heads), :] = jnp.full((own_heads, LANES), position_ref[q], jnp.int32)
    top_buf[...] = jnp.full(top_buf.shape, first_top, jnp.float32)
    sum_buf[...] = jnp.zeros(sum_buf.shape, jnp.float32)
    acc_buf[...] = jnp.zeros(acc_buf.shape, jnp.float32)
    for copy in own_copies:
        copy.wait()

    def absorb(j, xx, h):
        for step in range(1, sub_count):
            pair_arrival(j, xx, h, step).wait_recv()
        block = latent_buf[j, xx, :, pl.ds(h * cut, cut), :].reshape(unit, latent_width)
        rope_rows = rope_q_buf[:, pl.ds(heads_at, own_heads), :].reshape(rows, rope_width)
        rope_block = jnp.concatenate([rope_buf[j, xx, h, ss] for ss in range(sub_count)], axis=1)
        scores = lax.dot_general(
            query_buf[...].reshape(rows, latent_width), block,
            (((1,), (1,)), ((), ())), preferred_element_type=jnp.float32,
        )
        scores = (scores + jnp.dot(rope_rows, rope_block, preferred_element_type=jnp.float32)) * score_scale
        offsets = lax.broadcasted_iota(jnp.int32, (rows, LANES), 1)
        parts = []
        for ss in range(sub_count):
            root = (j * sect_count + xx) * sub_count + ss
            limit = jnp.minimum(length_ref[root] - h * cut, place_buf[...] - (root * token_count + h * cut - 1))
            for at in range(0, cut, LANES):
                part = scores[:, ss * cut + at:ss * cut + at + LANES]
                parts.append(jnp.where(offsets < limit - at, part, lowest_score))
        scores = jnp.concatenate(parts, axis=1)
        old_top = top_buf[...]
        new_top = jnp.maximum(old_top, jnp.max(scores, axis=1, keepdims=True))
        factor = jnp.exp2(old_top - new_top)
        weights = jnp.exp2(scores - spread(new_top, unit))
        sum_buf[...] = sum_buf[...] * factor + jnp.sum(weights, axis=1, keepdims=True)
        top_buf[...] = new_top
        acc_buf[...] = acc_buf[...] * spread(factor, latent_width) + jnp.dot(
            weights.astype(jnp.bfloat16), block, preferred_element_type=jnp.float32
        )

    def column_at(k, way):
        return z - k if way == 0 else z + k

    def inside(j):
        return (j >= 0) & (j < blk_count)

    def takes_side(k, h):
        return (k == 1) if h in side else False

    def pass_on(k, h):
        for way in range(2):
            j = column_at(k, way)
            target = z + 1 if way == 0 else z - 1

            @pl.when(inside(j))
            def _():
                here = held(j, x, s, h)
                z_copy(here, j, h, way, z).wait_recv()

                @pl.when(inside(target))
                def _():
                    z_copy(here, j, h, way, target).start()

                @pl.when(jnp.logical_not(takes_side(k, h)))
                def _():
                    for step in range(1, sect_count):
                        x_copy(here, j, h, step).start()
                to_pair(here, j, x, h)

    def take_sections(k, h):
        def one(j):
            for step in range(1, sect_count):
                x_arrival(j, h, step).wait_recv()
                xx = source_section(step)
                to_pair(held(j, xx, s, h), j, xx, h)

        for way in range(2):
            j = column_at(k, way)

            @pl.when(inside(j) & jnp.logical_not(takes_side(k, h)) & ((k > 0) | (way == 0)))
            def _():
                one(j)

    def absorb_at(k, h, mine, also_side=False):
        def one_way(way, carry):
            j = z + (2 * way - 1) * k
            here = inside(j) & ((k > 0) | (way == 0)) & (k >= 0)
            if not mine and h in side:
                here = here & ((k == 1) if also_side else (k != 1))

            @pl.when(here)
            def _():
                if mine:
                    absorb(j, x, h)
                else:
                    for step in range(1, sect_count):
                        absorb(j, source_section(step), h)
            return carry
        lax.fori_loop(0, 2, one_way, 0)

    def send_side(k):
        for way in range(2):
            target = z + 1 if way == 0 else z - 1
            behind = z if way == 0 else last_z - z

            @pl.when(inside(target) & (k == jnp.maximum(behind, 1)))
            def _():
                for h in side:
                    side_copy(z, h, way, target).start()

    def one_step(k, carry):
        for h in range(cuts):
            pass_on(k, h)
            take_sections(k - 1, h)
            absorb_at(k - 1, h, True)
            absorb_at(k - 2, h, False)
        send_side(k)
        return carry

    lax.fori_loop(1, blk_count, one_step, 0)
    for h in side:
        for way in range(2):
            j = column_at(1, way)

            @pl.when(inside(j))
            def _():
                side_copy(j, h, way, z).wait_recv()
                to_pair(held(j, other, s, h), j, other, h)
    for h in range(cuts):
        absorb_at(last_z, h, True)
    for h in range(cuts):
        if last_z > 0:
            absorb_at(last_z - 1, h, False)
    for h in side:
        absorb_at(1, h, False, also_side=True)
    for h in range(cuts):
        take_sections(last_z, h)
        absorb_at(last_z, h, False)

    weight_copy.wait()
    value_width = weight_hbm.shape[2]
    row_head = lax.rem(lax.broadcasted_iota(jnp.int32, (chunk_rows, value_width), 0), chunk_heads)

    def rows_of(value, c):
        width = value.shape[-1]
        part = value.reshape(query_count, own_heads, width)[:, c * chunk_heads:(c + 1) * chunk_heads, :]
        return part.reshape(chunk_rows, width)

    for c in range(chunk_count):
        inverse = 1.0 / rows_of(sum_buf[...], c)
        latent = (rows_of(acc_buf[...], c) * spread(inverse, latent_width)).astype(jnp.bfloat16)
        result = jnp.zeros((chunk_rows, value_width), jnp.float32)
        for h in range(0, chunk_heads, 2):
            pair = jnp.concatenate(
                [weight_buf[c * chunk_heads + h], weight_buf[c * chunk_heads + h + 1]], axis=1
            )
            both = jnp.dot(latent, pair, preferred_element_type=jnp.float32)
            result = jnp.where(row_head == h, both[:, :value_width], result)
            result = jnp.where(row_head == h + 1, both[:, value_width:], result)
        out_ref[:, c * chunk_heads:(c + 1) * chunk_heads, :] = result.reshape(
            query_count, chunk_heads, value_width
        ).astype(out_ref.dtype)

    def drain(j, carry):
        for h in range(cuts):
            @pl.when((j <= z) & (z < last_z))
            def _():
                z_copy(held(j, x, s, h), j, h, 0, z).wait_send()

            @pl.when((j >= z) & (z > 0))
            def _():
                z_copy(held(j, x, s, h), j, h, 1, z).wait_send()

            near = (j == z - 1) | (j == z + 1)

            @pl.when(jnp.logical_not(near if h in side else False))
            def _():
                for step in range(1, sect_count):
                    x_copy(held(j, x, s, h), j, h, step).wait_send()
            for xx in range(sect_count):
                for step in range(1, sub_count):
                    pair_copy(held(j, xx, s, h), j, xx, h, step).wait_send()
        return carry

    lax.fori_loop(0, blk_count, drain, 0)
    for h in side:
        @pl.when(z < last_z)
        def _():
            side_copy(z, h, 0, z).wait_send()

        @pl.when(z > 0)
        def _():
            side_copy(z, h, 1, z).wait_send()


def shards(query_latent, query_rope, cache_latent, cache_rope, lengths, positions, value_weight):
    query_count, head_count, latent_width = query_latent.shape
    rope_width = query_rope.shape[1]
    token_count = cache_latent.shape[1]
    blk_count, sect_count, sub_count = (lax.axis_size(name) for name in ("blk", "sect", "sub"))
    own_heads, _, value_width = value_weight.shape
    chunk_heads = min(16, own_heads)
    cuts = 2
    cut = token_count // cuts
    rows = query_count * own_heads
    peers = max(sect_count - 1, 1)
    pairs = max(sub_count - 1, 1)
    bf16, f32 = jnp.bfloat16, jnp.float32
    hbm = pl.BlockSpec(memory_space=pltpu.HBM)
    vmem = pl.BlockSpec(memory_space=pltpu.VMEM)
    dma = pltpu.SemaphoreType.DMA
    return pl.pallas_call(
        functools.partial(kernel, (blk_count, sect_count, sub_count, cuts, chunk_heads)),
        out_shape=jax.ShapeDtypeStruct((query_count, own_heads, value_width), bf16),
        in_specs=[hbm] * 7,
        out_specs=vmem,
        scratch_shapes=[
            pltpu.VMEM(query_rope.shape, bf16),
            pltpu.SMEM(lengths.shape, jnp.int32),
            pltpu.SMEM(positions.shape, jnp.int32),
            pltpu.VMEM((query_count, own_heads, latent_width), bf16),
            pltpu.VMEM((query_count, head_count, rope_width), bf16),
            pltpu.VMEM((blk_count, sect_count, sub_count, token_count, latent_width), bf16),
            pltpu.VMEM((blk_count, sect_count, cuts, sub_count, rope_width, cut), bf16),
            pltpu.VMEM((own_heads, latent_width, value_width), bf16),
            pltpu.VMEM((rows, LANES), jnp.int32),
            pltpu.VMEM((rows, LANES), f32),
            pltpu.VMEM((rows, LANES), f32),
            pltpu.VMEM((rows, latent_width), f32),
            dma((5 + 2 * cuts,)),
            dma((2, blk_count, cuts, 2)),
            dma((blk_count, cuts, 2)),
            dma((peers, blk_count, cuts, 2)),
            dma((peers, blk_count, cuts, 2)),
            dma((pairs, blk_count, sect_count, cuts, 2)),
            dma((pairs, blk_count, sect_count, cuts, 2)),
            dma((2, cuts, 2)),
            dma((2, cuts, 2)),
        ],
        compiler_params=pltpu.CompilerParams(
            collective_id=0, has_side_effects=True, vmem_limit_bytes=60 * 1024 * 1024
        ),
    )(query_latent, query_rope, cache_latent, cache_rope, lengths, positions, value_weight)


def solution(mesh):
    placed = (
        P(("rep", "blk"), None, None),
        P(("rep", "blk"), None, None),
        P(("rep", "blk", "sect", "sub"), None, None),
        P(("rep", "blk", "sect", "sub"), None, None),
        P("rep"),
        P(("rep", "blk")),
        P(("sect", "sub"), None, None),
    )
    return jax.shard_map(
        shards,
        mesh=mesh,
        in_specs=placed,
        out_specs=P(("rep", "blk"), ("sect", "sub"), None),
        check_vma=False,
    )
```

```python
import functools
import math

import jax
import jax.numpy as jnp
from jax import lax
from jax.experimental import pallas as pl
from jax.experimental.pallas import tpu as pltpu
from jax.sharding import PartitionSpec as P

lowest_score = -1e30
first_top = -1e29
LANES = 128
MESH = pl.DeviceIdType.MESH


def spread(column, width):
    return jnp.concatenate([column] * (width // LANES), axis=1)


def kernel(
    sizes, query_hbm, rope_q_hbm, latent_hbm, rope_hbm, length_hbm, position_hbm, weight_hbm,
    out_ref,
    rope_q_ref, length_ref, position_ref, rope_stage, query_buf, rope_q_buf, cache_buf, weight_buf, place_buf,
    top_buf, sum_buf, acc_buf,
    local_sem, z_send, z_recv, x_send, x_recv, pair_send, pair_recv, side_send, side_recv,
):
    blk_count, sect_count, sub_count, chunk_heads = sizes
    query_count, own_heads, latent_width = query_buf.shape
    rope_width = rope_q_hbm.shape[1]
    token_count = latent_hbm.shape[1]
    folds = latent_width // token_count
    rope_rows_count = rope_width // folds
    block_rows = rope_rows_count + token_count
    piece_count = 4
    step_rows = token_count // piece_count
    bounds = [0] + [rope_rows_count + (i + 1) * step_rows for i in range(piece_count)]
    rows = query_count * own_heads
    chunk_count = own_heads // chunk_heads
    chunk_rows = query_count * chunk_heads
    score_scale = math.log2(math.e) / math.sqrt(latent_width + rope_width)
    side = (2, 3) if sect_count == 2 else ()
    direct = tuple(p for p in range(piece_count) if p not in side)
    z = lax.axis_index("blk")
    x = lax.axis_index("sect")
    s = lax.axis_index("sub")
    last_z = blk_count - 1
    other = lax.rem(x + 1, sect_count)

    barrier = pltpu.get_barrier_semaphore()

    def greet(device_id):
        pl.semaphore_signal(barrier, inc=1, device_id=device_id, device_id_type=MESH)

    for step in range(1, sub_count):
        greet({"sub": lax.rem(s + step, sub_count)})
    for step in range(1, sect_count):
        greet({"sect": lax.rem(x + step, sect_count)})

    @pl.when(z > 0)
    def _():
        greet({"blk": z - 1})

    @pl.when(z < last_z)
    def _():
        greet({"blk": z + 1})

    heads_at = pl.multiple_of((x * sub_count + s) * own_heads, own_heads)
    own_copies = [
        pltpu.make_async_copy(
            latent_hbm.at[0], cache_buf.at[z, x, s, pl.ds(rope_rows_count, token_count)], local_sem.at[0]
        ),
        pltpu.make_async_copy(rope_hbm.at[0], rope_stage, local_sem.at[1]),
    ]
    small_copies = [
        pltpu.make_async_copy(source, landing, local_sem.at[2 + i])
        for i, (source, landing) in enumerate((
            (rope_q_hbm, rope_q_ref), (length_hbm, length_ref), (position_hbm, position_ref),
            (query_hbm.at[:, pl.ds(heads_at, own_heads), :], query_buf),
        ))
    ]
    weight_copy = pltpu.make_async_copy(weight_hbm, weight_buf, local_sem.at[6])
    for copy in own_copies + small_copies:
        copy.start()

    def place(j, xx, ss, first, end):
        return cache_buf.at[j, xx, ss, pl.ds(bounds[first], bounds[end] - bounds[first])]

    def send(j, xx, first, end, send_sem, recv_sem, device_id):
        here = place(j, xx, s, first, end)
        return pltpu.make_async_remote_copy(
            src_ref=here, dst_ref=here, send_sem=send_sem, recv_sem=recv_sem,
            device_id=device_id, device_id_type=MESH,
        )

    def arrival(j, xx, ss, first, end, recv_sem):
        here = place(j, xx, ss, first, end)
        return pltpu.make_async_remote_copy(
            src_ref=here, dst_ref=here, send_sem=recv_sem, recv_sem=recv_sem,
            device_id={"sub": s}, device_id_type=MESH,
        )

    def z_copy(j, p, way, target):
        return send(j, x, p, p + 1, z_send.at[way, j], z_recv.at[j, p], {"blk": target})

    def x_copy(j, p, step):
        return send(
            j, x, p, p + 1, x_send.at[step - 1, j], x_recv.at[step - 1, j, p],
            {"sect": lax.rem(x + step, sect_count)},
        )

    def source_section(step):
        return lax.rem(x + sect_count - step, sect_count)

    def source_sub(step):
        return lax.rem(s + sub_count - step, sub_count)

    def pair_copy(j, xx, p, step):
        return send(
            j, xx, p, p + 1, pair_send.at[step - 1, j, xx], pair_recv.at[step - 1, j, xx],
            {"sub": lax.rem(s + step, sub_count)},
        )

    def side_copy(j, way, target):
        return send(j, other, side[0], side[-1] + 1, side_send.at[way], side_recv.at[way], {"blk": target})

    def to_pair(j, xx, p):
        for step in range(1, sub_count):
            pair_copy(j, xx, p, step).start()

    neighbours = jnp.where(z > 0, 1, 0) + jnp.where(z < last_z, 1, 0)
    for copy in own_copies:
        copy.wait()
    for i in range(folds):
        cache_buf[z, x, s, 0:rope_rows_count, i * token_count:(i + 1) * token_count] = (
            rope_stage[i * rope_rows_count:(i + 1) * rope_rows_count, :]
        )
    pl.semaphore_wait(barrier, sub_count - 1 + sect_count - 1 + neighbours)

    for p in range(piece_count):
        @pl.when(z < last_z)
        def _():
            z_copy(z, p, 0, z + 1).start()

        @pl.when(z > 0)
        def _():
            z_copy(z, p, 1, z - 1).start()

        for step in range(1, sect_count):
            x_copy(z, p, step).start()
        to_pair(z, x, p)
    weight_copy.start()

    for copy in small_copies:
        copy.wait()
    for q in range(query_count):
        turned = jnp.transpose(rope_q_ref[q].astype(jnp.float32)).astype(jnp.bfloat16)
        rope_q_buf[q] = turned
        place_buf[pl.ds(q * own_heads, own_heads), :] = jnp.full((own_heads, LANES), position_ref[q], jnp.int32)
    top_buf[...] = jnp.full(top_buf.shape, first_top, jnp.float32)
    sum_buf[...] = jnp.zeros(sum_buf.shape, jnp.float32)
    acc_buf[...] = jnp.zeros(acc_buf.shape, jnp.float32)

    def absorb(j, xx):
        for step in range(1, sub_count):
            arrival(j, xx, source_sub(step), 0, piece_count, pair_recv.at[step - 1, j, xx]).wait_recv()
        queries = query_buf[...].reshape(rows, latent_width)
        rope_rows = rope_q_buf[:, pl.ds(heads_at, own_heads), :].reshape(rows, rope_width)
        offsets = lax.broadcasted_iota(jnp.int32, (rows, LANES), 1)
        parts = []
        for ss in range(sub_count):
            root = (j * sect_count + xx) * sub_count + ss
            block = cache_buf[j, xx, ss, rope_rows_count:block_rows, :]
            rope_block = jnp.concatenate([
                cache_buf[j, xx, ss, 0:rope_rows_count, i * token_count:(i + 1) * token_count] for i in range(folds)
            ], axis=0)
            scores = lax.dot_general(
                queries, block, (((1,), (1,)), ((), ())), preferred_element_type=jnp.float32,
            )
            scores = (scores + jnp.dot(rope_rows, rope_block, preferred_element_type=jnp.float32)) * score_scale
            limit = jnp.minimum(length_ref[root], place_buf[...] - (root * token_count - 1))
            for at in range(0, token_count, LANES):
                parts.append(jnp.where(offsets < limit - at, scores[:, at:at + LANES], lowest_score))
        old_top = top_buf[...]
        best = functools.reduce(jnp.maximum, parts)
        new_top = jnp.maximum(old_top, jnp.max(best, axis=1, keepdims=True))
        factor = jnp.exp2(old_top - new_top)
        weights = [jnp.exp2(part - new_top) for part in parts]
        sum_buf[...] = sum_buf[...] * factor + jnp.sum(sum(weights), axis=1, keepdims=True)
        top_buf[...] = new_top
        block = cache_buf[j, xx, :, rope_rows_count:block_rows, :].reshape(sub_count * token_count, latent_width)
        acc_buf[...] = acc_buf[...] * spread(factor, latent_width) + jnp.dot(
            jnp.concatenate([part.astype(jnp.bfloat16) for part in weights], axis=1), block,
            preferred_element_type=jnp.float32,
        )

    def column_at(k, way):
        return z - k if way == 0 else z + k

    def inside(j):
        return (j >= 0) & (j < blk_count)

    def by_x(k, p):
        return (k != 1) if p in side else (k == k)

    def pass_on(k, p):
        for way in range(2):
            j = column_at(k, way)
            target = z + 1 if way == 0 else z - 1

            @pl.when(inside(j))
            def _():
                arrival(j, x, s, p, p + 1, z_recv.at[j, p]).wait_recv()

                @pl.when(inside(target))
                def _():
                    z_copy(j, p, way, target).start()

                @pl.when(by_x(k, p))
                def _():
                    for step in range(1, sect_count):
                        x_copy(j, p, step).start()
                to_pair(j, x, p)

    def take_sections(k, p):
        for way in range(2):
            j = column_at(k, way)

            @pl.when(inside(j) & by_x(k, p) & ((k > 0) | (way == 0)))
            def _():
                for step in range(1, sect_count):
                    xx = source_section(step)
                    arrival(j, xx, s, p, p + 1, x_recv.at[step - 1, j, p]).wait_recv()
                    to_pair(j, xx, p)

    def absorb_at(k, mine):
        def one_way(way, carry):
            j = z + (2 * way - 1) * k

            @pl.when(inside(j) & ((k > 0) | (way == 0)) & (k >= 0))
            def _():
                if mine:
                    absorb(j, x)
                else:
                    for step in range(1, sect_count):
                        absorb(j, source_section(step))
            return carry
        lax.fori_loop(0, 2, one_way, 0)

    def send_side(k):
        for way in range(2):
            target = z + 1 if way == 0 else z - 1
            behind = z if way == 0 else last_z - z

            @pl.when(inside(target) & (k == jnp.maximum(behind, 1)))
            def _():
                side_copy(z, way, target).start()

    def one_step(k, carry):
        for p in range(piece_count):
            pass_on(k, p)
            take_sections(k - 1, p)
        if side:
            send_side(k)
        absorb_at(k - 1, True)
        absorb_at(jnp.where(k == 3, -1, k - 2) if side else k - 2, False)
        return carry

    lax.fori_loop(1, blk_count, one_step, 0)
    if side and blk_count > 1:
        for way in range(2):
            j = column_at(1, way)

            @pl.when(inside(j))
            def _():
                arrival(j, other, s, side[0], side[-1] + 1, side_recv.at[way]).wait_recv()
                for p in side:
                    to_pair(j, other, p)
    if blk_count > 1:
        absorb_at(last_z, True)
    if blk_count > 2 or not side:
        absorb_at(last_z - 1, False)
    if side and last_z > 2:
        absorb_at(1, False)
    for p in range(piece_count):
        take_sections(last_z, p)
    absorb_at(last_z, False)

    weight_copy.wait()
    value_width = weight_hbm.shape[2]
    row_head = lax.rem(lax.broadcasted_iota(jnp.int32, (chunk_rows, value_width), 0), chunk_heads)

    def rows_of(value, c):
        width = value.shape[-1]
        part = value.reshape(query_count, own_heads, width)[:, c * chunk_heads:(c + 1) * chunk_heads, :]
        return part.reshape(chunk_rows, width)

    for c in range(chunk_count):
        inverse = 1.0 / rows_of(sum_buf[...], c)
        latent = (rows_of(acc_buf[...], c) * spread(inverse, latent_width)).astype(jnp.bfloat16)
        result = jnp.zeros((chunk_rows, value_width), jnp.float32)
        for h in range(0, chunk_heads, 2):
            pair = jnp.concatenate(
                [weight_buf[c * chunk_heads + h], weight_buf[c * chunk_heads + h + 1]], axis=1
            )
            both = jnp.dot(latent, pair, preferred_element_type=jnp.float32)
            result = jnp.where(row_head == h, both[:, :value_width], result)
            result = jnp.where(row_head == h + 1, both[:, value_width:], result)
        out_ref[:, c * chunk_heads:(c + 1) * chunk_heads, :] = result.reshape(
            query_count, chunk_heads, value_width
        ).astype(out_ref.dtype)

    def drain(j, carry):
        whole_copy = lambda xx, sem: send(j, xx, 0, piece_count, sem, sem, {"sub": s})

        @pl.when((j <= z) & (z < last_z))
        def _():
            whole_copy(x, z_send.at[0, j]).wait_send()

        @pl.when((j >= z) & (z > 0))
        def _():
            whole_copy(x, z_send.at[1, j]).wait_send()

        near = ((j == z - 1) | (j == z + 1)) if side else (j < 0)
        for step in range(1, sect_count):
            @pl.when(near)
            def _():
                send(j, x, direct[0], direct[-1] + 1, x_send.at[step - 1, j], x_send.at[step - 1, j], {"sub": s}).wait_send()

            @pl.when(jnp.logical_not(near))
            def _():
                whole_copy(x, x_send.at[step - 1, j]).wait_send()
        for xx in range(sect_count):
            for step in range(1, sub_count):
                whole_copy(xx, pair_send.at[step - 1, j, xx]).wait_send()
        return carry

    lax.fori_loop(0, blk_count, drain, 0)
    if side:
        @pl.when(z < last_z)
        def _():
            side_copy(z, 0, z).wait_send()

        @pl.when(z > 0)
        def _():
            side_copy(z, 1, z).wait_send()


def shards(query_latent, query_rope, cache_latent, cache_rope, lengths, positions, value_weight):
    query_count, head_count, latent_width = query_latent.shape
    rope_width = query_rope.shape[1]
    token_count = cache_latent.shape[1]
    blk_count, sect_count, sub_count = (lax.axis_size(name) for name in ("blk", "sect", "sub"))
    own_heads, _, value_width = value_weight.shape
    chunk_heads = min(16, own_heads)
    block_rows = token_count + rope_width * token_count // latent_width
    rows = query_count * own_heads
    peers = max(sect_count - 1, 1)
    pairs = max(sub_count - 1, 1)
    bf16, f32 = jnp.bfloat16, jnp.float32
    hbm = pl.BlockSpec(memory_space=pltpu.HBM)
    vmem = pl.BlockSpec(memory_space=pltpu.VMEM)
    dma = pltpu.SemaphoreType.DMA
    return pl.pallas_call(
        functools.partial(kernel, (blk_count, sect_count, sub_count, chunk_heads)),
        out_shape=pltpu.VMEM((query_count, own_heads, value_width), bf16),
        in_specs=[hbm] * 7,
        out_specs=vmem,
        scratch_shapes=[
            pltpu.VMEM(query_rope.shape, bf16),
            pltpu.SMEM(lengths.shape, jnp.int32),
            pltpu.SMEM(positions.shape, jnp.int32),
            pltpu.VMEM((rope_width, token_count), bf16),
            pltpu.VMEM((query_count, own_heads, latent_width), bf16),
            pltpu.VMEM((query_count, head_count, rope_width), bf16),
            pltpu.VMEM((blk_count, sect_count, sub_count, block_rows, latent_width), bf16),
            pltpu.VMEM((own_heads, latent_width, value_width), bf16),
            pltpu.VMEM((rows, LANES), jnp.int32),
            pltpu.VMEM((rows, LANES), f32),
            pltpu.VMEM((rows, LANES), f32),
            pltpu.VMEM((rows, latent_width), f32),
            dma((7,)),
            dma((2, blk_count)),
            dma((blk_count, 4)),
            dma((peers, blk_count)),
            dma((peers, blk_count, 4)),
            dma((pairs, blk_count, sect_count)),
            dma((pairs, blk_count, sect_count)),
            dma((2,)),
            dma((2,)),
        ],
        compiler_params=pltpu.CompilerParams(
            collective_id=0, has_side_effects=True, vmem_limit_bytes=60 * 1024 * 1024
        ),
    )(query_latent, query_rope, cache_latent, cache_rope, lengths, positions, value_weight)


def solution(mesh):
    placed = (
        P(("rep", "blk"), None, None),
        P(("rep", "blk"), None, None),
        P(("rep", "blk", "sect", "sub"), None, None),
        P(("rep", "blk", "sect", "sub"), None, None),
        P("rep"),
        P(("rep", "blk")),
        P(("sect", "sub"), None, None),
    )
    return jax.shard_map(
        shards,
        mesh=mesh,
        in_specs=placed,
        out_specs=P(("rep", "blk"), ("sect", "sub"), None),
        check_vma=False,
    )
```

```python
import functools
import math

import jax
import jax.numpy as jnp
from jax import lax
from jax.experimental import pallas as pl
from jax.experimental.pallas import tpu as pltpu
from jax.sharding import PartitionSpec as P

lowest_score = -1e30
first_top = -1e29
LANES = 128
PIECES = 4
MESH = pl.DeviceIdType.MESH


def spread(column, width):
    return jnp.concatenate([column] * (width // LANES), axis=1)


def kernel(
    sizes, query_hbm, rope_q_hbm, latent_hbm, rope_hbm, length_hbm, position_hbm, weight_hbm,
    out_ref,
    rope_q_ref, length_ref, position_ref, rope_stage, query_buf, rope_q_buf, rope_rows_buf, cache_buf, weight_buf,
    mark_buf, place_buf, top_buf, sum_buf, acc_buf, result_buf, part_buf, stat_buf,
    local_sem, z_send, z_recv, x_send, x_recv, pair_send, pair_recv, side_send, side_recv,
    lend_send, lend_recv, part_send, part_recv,
):
    blk_count, sect_count, sub_count, chunk_heads = sizes
    _, query_count, own_heads, latent_width = query_buf.shape
    rope_width = rope_q_hbm.shape[1]
    token_count = latent_hbm.shape[1]
    value_width = weight_hbm.shape[2]
    folds = latent_width // token_count
    rope_rows_count = rope_width // folds
    block_rows = rope_rows_count + token_count
    step_rows = token_count // PIECES
    bounds = [0] + [rope_rows_count + (i + 1) * step_rows for i in range(PIECES)]
    rows = query_count * own_heads
    chunk_count = own_heads // chunk_heads
    chunk_rows = query_count * chunk_heads
    score_scale = math.log2(math.e) / math.sqrt(latent_width + rope_width)
    z = lax.axis_index("blk")
    x = lax.axis_index("sect")
    s = lax.axis_index("sub")
    last_z = blk_count - 1
    other = lax.rem(x + 1, sect_count)
    at_end = (z == 0) | (z == last_z)
    side = sect_count == 2
    lend = blk_count >= 4
    steps = last_z - 1 if lend else last_z
    helper = ((z == 1) | (z == last_z - 1)) if lend else (z < 0)

    barrier = pltpu.get_barrier_semaphore()

    def greet(device_id):
        pl.semaphore_signal(barrier, inc=1, device_id=device_id, device_id_type=MESH)

    for step in range(1, sub_count):
        greet({"sub": lax.rem(s + step, sub_count)})
    for step in range(1, sect_count):
        greet({"sect": lax.rem(x + step, sect_count)})

    @pl.when(z > 0)
    def _():
        greet({"blk": z - 1})

    @pl.when(z < last_z)
    def _():
        greet({"blk": z + 1})

    heads_at = pl.multiple_of((x * sub_count + s) * own_heads, own_heads)
    own_copies = [
        pltpu.make_async_copy(
            latent_hbm.at[0], cache_buf.at[z, x, s, pl.ds(rope_rows_count, token_count)], local_sem.at[0]
        ),
        pltpu.make_async_copy(rope_hbm.at[0], rope_stage, local_sem.at[1]),
    ]
    small_copies = [
        pltpu.make_async_copy(source, landing, local_sem.at[2 + i])
        for i, (source, landing) in enumerate((
            (rope_q_hbm, rope_q_ref), (length_hbm, length_ref), (position_hbm, position_ref),
            (query_hbm.at[:, pl.ds(heads_at, own_heads), :], query_buf.at[0]),
        ))
    ]
    weight_copy = pltpu.make_async_copy(weight_hbm, weight_buf, local_sem.at[6])
    for copy in own_copies + small_copies:
        copy.start()

    def send(source, landing, send_sem, recv_sem, device_id):
        return pltpu.make_async_remote_copy(
            src_ref=source, dst_ref=landing, send_sem=send_sem, recv_sem=recv_sem,
            device_id=device_id, device_id_type=MESH,
        )

    def place(j, xx, ss, first, end):
        return cache_buf.at[j, xx, ss, pl.ds(bounds[first], bounds[end] - bounds[first])]

    def block_send(j, xx, first, end, send_sem, recv_sem, device_id):
        here = place(j, xx, s, first, end)
        return send(here, here, send_sem, recv_sem, device_id)

    def await_block(j, xx, ss, first, end, recv_sem):
        here = place(j, xx, ss, first, end)
        send(here, here, recv_sem, recv_sem, {"sub": s}).wait_recv()

    def z_copy(j, p, way, target):
        return block_send(j, x, p, p + 1, z_send.at[way, j], z_recv.at[j, p], {"blk": target})

    def x_copy(j, p, step):
        return block_send(
            j, x, p, p + 1, x_send.at[step - 1, j], x_recv.at[step - 1, j, p],
            {"sect": lax.rem(x + step, sect_count)},
        )

    def source_section(step):
        return lax.rem(x + sect_count - step, sect_count)

    def source_sub(step):
        return lax.rem(s + sub_count - step, sub_count)

    def to_pair(j, xx, first, end):
        for step in range(1, sub_count):
            block_send(
                j, xx, first, end, pair_send.at[step - 1, j, xx], pair_recv.at[step - 1, j, xx],
                {"sub": lax.rem(s + step, sub_count)},
            ).start()

    def side_copy(j, way, target, first):
        return block_send(j, other, first, PIECES, side_send.at[way], side_recv.at[way], {"blk": target})

    inward = jnp.where(z == 0, 1, last_z - 1)
    outward = jnp.where(z == 1, 0, last_z)
    lend_copies = [
        send(ref.at[0], ref.at[1], lend_send.at[i], lend_recv.at[i], {"blk": inward})
        for i, ref in enumerate((query_buf, rope_rows_buf, mark_buf))
    ]

    def part_copies(c):
        return [
            send(ref.at[0, c], ref.at[1, c], part_send.at[c, i], part_recv.at[c, i], {"blk": outward})
            for i, ref in enumerate((part_buf, stat_buf))
        ]

    neighbours = jnp.where(z > 0, 1, 0) + jnp.where(z < last_z, 1, 0)
    for copy in own_copies:
        copy.wait()
    for i in range(folds):
        cache_buf[z, x, s, 0:rope_rows_count, i * token_count:(i + 1) * token_count] = (
            rope_stage[i * rope_rows_count:(i + 1) * rope_rows_count, :]
        )
    pl.semaphore_wait(barrier, sub_count - 1 + sect_count - 1 + neighbours)

    for p in range(PIECES):
        @pl.when(z < last_z)
        def _():
            z_copy(z, p, 0, z + 1).start()

        @pl.when(z > 0)
        def _():
            z_copy(z, p, 1, z - 1).start()

        for step in range(1, sect_count):
            x_copy(z, p, step).start()
        to_pair(z, x, p, p + 1)

    for copy in small_copies:
        copy.wait()
    for q in range(query_count):
        rope_q_buf[q] = jnp.transpose(rope_q_ref[q].astype(jnp.float32)).astype(jnp.bfloat16)
        mark_buf[0, q:q + 1, :] = jnp.full((1, LANES), position_ref[q], jnp.int32)
    rope_rows_buf[0] = rope_q_buf[:, pl.ds(heads_at, own_heads), :]
    if lend:
        @pl.when(at_end)
        def _():
            for copy in lend_copies:
                copy.start()
    weight_copy.start()

    def set_places(g):
        for q in range(query_count):
            place_buf[g, pl.ds(q * own_heads, own_heads), :] = jnp.broadcast_to(
                mark_buf[g, q:q + 1, :], (own_heads, LANES)
            )

    set_places(0)
    top_buf[...] = jnp.full(top_buf.shape, first_top, jnp.float32)
    sum_buf[...] = jnp.zeros(sum_buf.shape, jnp.float32)
    acc_buf[...] = jnp.zeros(acc_buf.shape, jnp.float32)

    def await_pair(j, xx):
        for step in range(1, sub_count):
            await_block(j, xx, source_sub(step), 0, PIECES, pair_recv.at[step - 1, j, xx])

    def absorb(j, xx, g):
        queries = query_buf[g].reshape(rows, latent_width)
        rope_rows = rope_rows_buf[g].reshape(rows, rope_width)
        offsets = lax.broadcasted_iota(jnp.int32, (rows, LANES), 1)
        parts = []
        for ss in range(sub_count):
            root = (j * sect_count + xx) * sub_count + ss
            block = cache_buf[j, xx, ss, rope_rows_count:block_rows, :]
            rope_block = jnp.concatenate([
                cache_buf[j, xx, ss, 0:rope_rows_count, i * token_count:(i + 1) * token_count] for i in range(folds)
            ], axis=0)
            scores = lax.dot_general(
                queries, block, (((1,), (1,)), ((), ())), preferred_element_type=jnp.float32,
            )
            scores = (scores + jnp.dot(rope_rows, rope_block, preferred_element_type=jnp.float32)) * score_scale
            limit = jnp.minimum(length_ref[root], place_buf[g] - (root * token_count - 1))
            for at in range(0, token_count, LANES):
                parts.append(jnp.where(offsets < limit - at, scores[:, at:at + LANES], lowest_score))
        old_top = top_buf[g]
        best = functools.reduce(jnp.maximum, parts)
        new_top = jnp.maximum(old_top, jnp.max(best, axis=1, keepdims=True))
        factor = jnp.exp2(old_top - new_top)
        weights = [jnp.exp2(part - new_top) for part in parts]
        sum_buf[g] = sum_buf[g] * factor + jnp.sum(sum(weights), axis=1, keepdims=True)
        top_buf[g] = new_top
        block = cache_buf[j, xx, :, rope_rows_count:block_rows, :].reshape(sub_count * token_count, latent_width)
        acc_buf[g] = acc_buf[g] * spread(factor, latent_width) + jnp.dot(
            jnp.concatenate([part.astype(jnp.bfloat16) for part in weights], axis=1), block,
            preferred_element_type=jnp.float32,
        )

    def inside(j):
        return (j >= 0) & (j < blk_count)

    def by_x(k, p):
        if not side or p == 0:
            return k == k
        return (k != 1) | at_end if p == 1 else k != 1

    def pass_on(k, p):
        for way in range(2):
            j = z - k if way == 0 else z + k
            target = z + 1 if way == 0 else z - 1

            @pl.when(inside(j))
            def _():
                await_block(j, x, s, p, p + 1, z_recv.at[j, p])

                @pl.when(inside(target) & ((k + 1 != last_z) if lend else (k == k)))
                def _():
                    z_copy(j, p, way, target).start()

                @pl.when(by_x(k, p))
                def _():
                    for step in range(1, sect_count):
                        x_copy(j, p, step).start()
                to_pair(j, x, p, p + 1)

    def take_sections(k, p):
        for way in range(2):
            j = z - k if way == 0 else z + k

            @pl.when(inside(j) & by_x(k, p) & ((k > 0) | (way == 0)))
            def _():
                for step in range(1, sect_count):
                    xx = source_section(step)
                    await_block(j, xx, s, p, p + 1, x_recv.at[step - 1, j, p])
                    to_pair(j, xx, p, p + 1)

    def absorb_at(k, mine, ways=(0, 1), g=0):
        def one_way(way, carry):
            j = z + (2 * way - 1) * k

            @pl.when(inside(j) & ((k > 0) | (way == 0)))
            def _():
                if mine:
                    if g == 0:
                        await_pair(j, x)
                    absorb(j, x, g)
                else:
                    for step in range(1, sect_count):
                        if g == 0:
                            await_pair(j, source_section(step))
                        absorb(j, source_section(step), g)
            return carry
        lax.fori_loop(ways[0], ways[-1] + 1, one_way, 0)

    def first_side(way_target):
        return (way_target == 0) | (way_target == last_z)

    def send_side():
        for way in range(2):
            target = z + 1 if way == 0 else z - 1
            for first in (1, 2):
                @pl.when(inside(target) & (first_side(target) == (first == 2)))
                def _():
                    side_copy(z, way, target, first).start()

    def take_side():
        for way in range(2):
            j = z - 1 if way == 0 else z + 1
            for first in (1, 2):
                @pl.when(inside(j) & (at_end == (first == 2)))
                def _():
                    await_block(j, other, s, first, PIECES, side_recv.at[way])
                    to_pair(j, other, first, PIECES)

    absorb_at(0, True, ways=(0,))
    if blk_count > 1:
        for p in range(PIECES):
            pass_on(1, p)
            take_sections(0, p)
        if side:
            send_side()
    else:
        for p in range(PIECES):
            take_sections(0, p)

    def one_step(k, carry):
        for p in range(PIECES):
            pass_on(k, p)
            if p > 0:
                take_sections(k - 1, p - 1)
            if p == 0:
                absorb_at(k - 1, True, ways=(0,))
            if p == 1:
                absorb_at(k - 1, True, ways=(1,))
            if p == 2:
                @pl.when((k != 3) if side else (k == k))
                def _():
                    absorb_at(k - 2, False)
        take_sections(k - 1, PIECES - 1)
        return carry

    if steps > 1:
        lax.fori_loop(2, steps + 1, one_step, 0)

    row_head = lax.rem(lax.broadcasted_iota(jnp.int32, (chunk_rows, value_width), 0), chunk_heads)

    def rows_of(value, c):
        width = value.shape[-1]
        part = value.reshape(query_count, own_heads, width)[:, c * chunk_heads:(c + 1) * chunk_heads, :]
        return part.reshape(chunk_rows, width)

    def project(g, c):
        latent = rows_of(acc_buf[g], c).astype(jnp.bfloat16)
        result = jnp.zeros((chunk_rows, value_width), jnp.float32)
        for h in range(0, chunk_heads, 2):
            pair = jnp.concatenate(
                [weight_buf[c * chunk_heads + h], weight_buf[c * chunk_heads + h + 1]], axis=1
            )
            both = jnp.dot(latent, pair, preferred_element_type=jnp.float32)
            result = jnp.where(row_head == h, both[:, :value_width], result)
            result = jnp.where(row_head == h + 1, both[:, value_width:], result)
        return result

    if lend:
        @pl.when(helper)
        def _():
            for copy in lend_copies:
                copy.wait_recv()
            set_places(1)
    if steps > 0:
        for p in range(PIECES):
            take_sections(steps, p)
            if p == 0:
                absorb_at(steps, True)
            if p == 1 and lend:
                @pl.when(helper)
                def _():
                    absorb_at(steps, True, g=1)
    weight_copy.wait()
    if steps > 0 and side:
        take_side()
    if steps > 0:
        absorb_at(steps, False)
    if lend:
        @pl.when(helper)
        def _():
            absorb_at(steps, False, g=1)
            for c in range(chunk_count):
                part_buf[0, c] = project(1, c).astype(jnp.bfloat16)
                stat_buf[0, c, 0:8] = jnp.transpose(rows_of(top_buf[1], c))[0:8]
                stat_buf[0, c, 8:16] = jnp.transpose(rows_of(sum_buf[1], c))[0:8]
                for copy in part_copies(c):
                    copy.start()
    if steps - 1 >= 2 or not side and steps >= 1 or steps == 1:
        absorb_at(steps - 1, False)
    if side and steps >= 2:
        absorb_at(1, False)

    def drain(j, carry):
        def whole_wait(xx, sem):
            block_send(j, xx, 0, PIECES, sem, sem, {"sub": s}).wait_send()

        far_up = ((j == 0) & (z + 1 == last_z)) if lend else (j < 0)
        far_down = ((j == last_z) & (z == 1)) if lend else (j < 0)
        here = ((j - z != last_z) & (z - j != last_z)) if lend else (j >= 0)

        @pl.when((j <= z) & (z < last_z) & jnp.logical_not(far_up))
        def _():
            whole_wait(x, z_send.at[0, j])

        @pl.when((j >= z) & (z > 0) & jnp.logical_not(far_down))
        def _():
            whole_wait(x, z_send.at[1, j])

        near = ((j == z - 1) | (j == z + 1)) if side else (j < 0)
        for step in range(1, sect_count):
            sem = x_send.at[step - 1, j]
            for end in (1, 2):
                @pl.when(near & (at_end == (end == 2)))
                def _():
                    block_send(j, x, 0, end, sem, sem, {"sub": s}).wait_send()

            @pl.when(here & jnp.logical_not(near))
            def _():
                whole_wait(x, sem)

        @pl.when(here)
        def _():
            for xx in range(sect_count):
                for step in range(1, sub_count):
                    whole_wait(xx, pair_send.at[step - 1, j, xx])
        return carry

    lax.fori_loop(0, blk_count, drain, 0)
    if side:
        for way in range(2):
            target = z + 1 if way == 0 else z - 1
            for first in (1, 2):
                @pl.when(inside(target) & (first_side(target) == (first == 2)))
                def _():
                    side_copy(z, way, z, first).wait_send()

    for c in range(chunk_count):
        result_buf[c] = project(0, c)

    def write(c, value):
        out_ref[:, c * chunk_heads:(c + 1) * chunk_heads, :] = value.reshape(
            query_count, chunk_heads, value_width
        ).astype(out_ref.dtype)

    merged = at_end if lend else (z < 0)

    @pl.when(jnp.logical_not(merged))
    def _():
        for c in range(chunk_count):
            write(c, result_buf[c] / rows_of(sum_buf[0], c))

    if lend:
        @pl.when(at_end)
        def _():
            for copy in lend_copies:
                copy.wait_send()
            for c in range(chunk_count):
                for copy in part_copies(c):
                    copy.wait_recv()
                top, total = rows_of(top_buf[0], c), rows_of(sum_buf[0], c)
                stat = stat_buf[1, c]
                far_top = jnp.transpose(jnp.broadcast_to(stat[0:1], (LANES, chunk_rows)))
                far_total = jnp.transpose(jnp.broadcast_to(stat[8:9], (LANES, chunk_rows)))
                overall = jnp.maximum(top, far_top)
                factor, far_factor = jnp.exp2(top - overall), jnp.exp2(far_top - overall)
                value = result_buf[c] * factor + part_buf[1, c].astype(jnp.float32) * far_factor
                write(c, value / (total * factor + far_total * far_factor))

        @pl.when(helper)
        def _():
            for c in range(chunk_count):
                for copy in part_copies(c):
                    copy.wait_send()


def shards(query_latent, query_rope, cache_latent, cache_rope, lengths, positions, value_weight):
    query_count, head_count, latent_width = query_latent.shape
    rope_width = query_rope.shape[1]
    token_count = cache_latent.shape[1]
    blk_count, sect_count, sub_count = (lax.axis_size(name) for name in ("blk", "sect", "sub"))
    own_heads, _, value_width = value_weight.shape
    chunk_heads = min(16, own_heads)
    chunk_count = own_heads // chunk_heads
    chunk_rows = query_count * chunk_heads
    block_rows = token_count + rope_width * token_count // latent_width
    rows = query_count * own_heads
    peers = max(sect_count - 1, 1)
    pairs = max(sub_count - 1, 1)
    bf16, f32 = jnp.bfloat16, jnp.float32
    hbm = pl.BlockSpec(memory_space=pltpu.HBM)
    vmem = pl.BlockSpec(memory_space=pltpu.VMEM)
    dma = pltpu.SemaphoreType.DMA
    return pl.pallas_call(
        functools.partial(kernel, (blk_count, sect_count, sub_count, chunk_heads)),
        out_shape=pltpu.VMEM((query_count, own_heads, value_width), bf16),
        in_specs=[hbm] * 7,
        out_specs=vmem,
        scratch_shapes=[
            pltpu.VMEM(query_rope.shape, bf16),
            pltpu.SMEM(lengths.shape, jnp.int32),
            pltpu.SMEM(positions.shape, jnp.int32),
            pltpu.VMEM((rope_width, token_count), bf16),
            pltpu.VMEM((2, query_count, own_heads, latent_width), bf16),
            pltpu.VMEM((query_count, head_count, rope_width), bf16),
            pltpu.VMEM((2, query_count, own_heads, rope_width), bf16),
            pltpu.VMEM((blk_count, sect_count, sub_count, block_rows, latent_width), bf16),
            pltpu.VMEM((own_heads, latent_width, value_width), bf16),
            pltpu.VMEM((2, query_count, LANES), jnp.int32),
            pltpu.VMEM((2, rows, LANES), jnp.int32),
            pltpu.VMEM((2, rows, LANES), f32),
            pltpu.VMEM((2, rows, LANES), f32),
            pltpu.VMEM((2, rows, latent_width), f32),
            pltpu.VMEM((chunk_count, chunk_rows, value_width), f32),
            pltpu.VMEM((2, chunk_count, chunk_rows, value_width), bf16),
            pltpu.VMEM((2, chunk_count, 16, chunk_rows), f32),
            dma((7,)),
            dma((2, blk_count)),
            dma((blk_count, PIECES)),
            dma((peers, blk_count)),
            dma((peers, blk_count, PIECES)),
            dma((pairs, blk_count, sect_count)),
            dma((pairs, blk_count, sect_count)),
            dma((2,)),
            dma((2,)),
            dma((3,)),
            dma((3,)),
            dma((chunk_count, 2)),
            dma((chunk_count, 2)),
        ],
        compiler_params=pltpu.CompilerParams(
            collective_id=0, has_side_effects=True, vmem_limit_bytes=60 * 1024 * 1024
        ),
    )(query_latent, query_rope, cache_latent, cache_rope, lengths, positions, value_weight)


def solution(mesh):
    placed = (
        P(("rep", "blk"), None, None),
        P(("rep", "blk"), None, None),
        P(("rep", "blk", "sect", "sub"), None, None),
        P(("rep", "blk", "sect", "sub"), None, None),
        P("rep"),
        P(("rep", "blk")),
        P(("sect", "sub"), None, None),
    )
    return jax.shard_map(
        shards,
        mesh=mesh,
        in_specs=placed,
        out_specs=P(("rep", "blk"), ("sect", "sub"), None),
        check_vma=False,
    )
```

```python
import functools
import math

import jax
import jax.numpy as jnp
from jax import lax
from jax.experimental import pallas as pl
from jax.experimental.pallas import tpu as pltpu
from jax.sharding import PartitionSpec as P

lowest_score = -1e30
first_top = -1e29
LANES = 128
PIECES = 4
MESH = pl.DeviceIdType.MESH


def spread(column, width):
    return jnp.concatenate([column] * (width // LANES), axis=1)


def kernel(
    sizes, query_hbm, rope_q_hbm, latent_hbm, rope_hbm, length_hbm, position_hbm, weight_hbm,
    out_ref,
    rope_q_ref, length_ref, position_ref, rope_stage, query_buf, rope_q_buf, rope_rows_buf, cache_buf, weight_buf,
    mark_buf, place_buf, top_buf, sum_buf, acc_buf, result_buf, part_buf, stat_buf,
    local_sem, z_send, z_recv, x_send, x_recv, pair_send, pair_recv, side_send, side_recv,
    lend_send, lend_recv, part_send, part_recv,
):
    blk_count, sect_count, sub_count, chunk_heads = sizes
    _, query_count, own_heads, latent_width = query_buf.shape
    rope_width = rope_q_hbm.shape[1]
    token_count = latent_hbm.shape[1]
    value_width = weight_hbm.shape[2]
    folds = latent_width // token_count
    rope_rows_count = rope_width // folds
    block_rows = rope_rows_count + token_count
    step_rows = token_count // PIECES
    bounds = [0] + [rope_rows_count + (i + 1) * step_rows for i in range(PIECES)]
    rows = query_count * own_heads
    chunk_count = own_heads // chunk_heads
    chunk_rows = query_count * chunk_heads
    score_scale = math.log2(math.e) / math.sqrt(latent_width + rope_width)
    z = lax.axis_index("blk")
    x = lax.axis_index("sect")
    s = lax.axis_index("sub")
    last_z = blk_count - 1
    other = lax.rem(x + 1, sect_count)
    at_end = (z == 0) | (z == last_z)
    side = sect_count == 2
    lend = blk_count >= 4
    steps = last_z - 1 if lend else last_z
    helper = ((z == 1) | (z == last_z - 1)) if lend else (z < 0)

    barrier = pltpu.get_barrier_semaphore()

    def greet(device_id):
        pl.semaphore_signal(barrier, inc=1, device_id=device_id, device_id_type=MESH)

    for step in range(1, sub_count):
        greet({"sub": lax.rem(s + step, sub_count)})
    for step in range(1, sect_count):
        greet({"sect": lax.rem(x + step, sect_count)})

    @pl.when(z > 0)
    def _():
        greet({"blk": z - 1})

    @pl.when(z < last_z)
    def _():
        greet({"blk": z + 1})

    heads_at = pl.multiple_of((x * sub_count + s) * own_heads, own_heads)
    own_copies = [
        pltpu.make_async_copy(
            latent_hbm.at[0], cache_buf.at[z, x, s, pl.ds(rope_rows_count, token_count)], local_sem.at[0]
        ),
        pltpu.make_async_copy(rope_hbm.at[0], rope_stage, local_sem.at[1]),
    ]
    small_copies = [
        pltpu.make_async_copy(source, landing, local_sem.at[2 + i])
        for i, (source, landing) in enumerate((
            (rope_q_hbm, rope_q_ref), (length_hbm, length_ref), (position_hbm, position_ref),
            (query_hbm.at[:, pl.ds(heads_at, own_heads), :], query_buf.at[0]),
        ))
    ]
    weight_copy = pltpu.make_async_copy(weight_hbm, weight_buf, local_sem.at[6])
    for copy in own_copies + small_copies:
        copy.start()

    def send(source, landing, send_sem, recv_sem, device_id):
        return pltpu.make_async_remote_copy(
            src_ref=source, dst_ref=landing, send_sem=send_sem, recv_sem=recv_sem,
            device_id=device_id, device_id_type=MESH,
        )

    def place(j, xx, ss, first, end):
        return cache_buf.at[j, xx, ss, pl.ds(bounds[first], bounds[end] - bounds[first])]

    def block_send(j, xx, first, end, send_sem, recv_sem, device_id):
        here = place(j, xx, s, first, end)
        return send(here, here, send_sem, recv_sem, device_id)

    def await_block(j, xx, ss, first, end, recv_sem):
        here = place(j, xx, ss, first, end)
        send(here, here, recv_sem, recv_sem, {"sub": s}).wait_recv()

    def z_copy(j, p, way, target):
        return block_send(j, x, p, p + 1, z_send.at[way, j], z_recv.at[j, p], {"blk": target})

    def x_copy(j, p, step):
        return block_send(
            j, x, p, p + 1, x_send.at[step - 1, j], x_recv.at[step - 1, j, p],
            {"sect": lax.rem(x + step, sect_count)},
        )

    def source_section(step):
        return lax.rem(x + sect_count - step, sect_count)

    def source_sub(step):
        return lax.rem(s + sub_count - step, sub_count)

    def to_pair(j, xx, first, end):
        for step in range(1, sub_count):
            block_send(
                j, xx, first, end, pair_send.at[step - 1, j, xx], pair_recv.at[step - 1, j, xx],
                {"sub": lax.rem(s + step, sub_count)},
            ).start()

    def side_copy(j, way, target, first):
        return block_send(j, other, first, PIECES, side_send.at[way], side_recv.at[way], {"blk": target})

    inward = jnp.where(z == 0, 1, last_z - 1)
    outward = jnp.where(z == 1, 0, last_z)
    lend_copies = [
        send(ref.at[0], ref.at[1], lend_send.at[i], lend_recv.at[i], {"blk": inward})
        for i, ref in enumerate((query_buf, rope_rows_buf, mark_buf))
    ]

    def part_copies(c):
        return [
            send(ref.at[0, c], ref.at[1, c], part_send.at[c, i], part_recv.at[c, i], {"blk": outward})
            for i, ref in enumerate((part_buf, stat_buf))
        ]

    neighbours = jnp.where(z > 0, 1, 0) + jnp.where(z < last_z, 1, 0)
    for copy in own_copies:
        copy.wait()
    for i in range(folds):
        cache_buf[z, x, s, 0:rope_rows_count, i * token_count:(i + 1) * token_count] = (
            rope_stage[i * rope_rows_count:(i + 1) * rope_rows_count, :]
        )
    pl.semaphore_wait(barrier, sub_count - 1 + sect_count - 1 + neighbours)

    for p in range(PIECES):
        @pl.when(z < last_z)
        def _():
            z_copy(z, p, 0, z + 1).start()

        @pl.when(z > 0)
        def _():
            z_copy(z, p, 1, z - 1).start()

        for step in range(1, sect_count):
            x_copy(z, p, step).start()
        to_pair(z, x, p, p + 1)

    for copy in small_copies:
        copy.wait()
    for q in range(query_count):
        rope_q_buf[q] = jnp.transpose(rope_q_ref[q].astype(jnp.float32)).astype(jnp.bfloat16)
        mark_buf[0, q:q + 1, :] = jnp.full((1, LANES), position_ref[q], jnp.int32)
    rope_rows_buf[0] = rope_q_buf[:, pl.ds(heads_at, own_heads), :]
    if lend:
        @pl.when(at_end)
        def _():
            for copy in lend_copies:
                copy.start()
    weight_copy.start()

    def set_places(g):
        for q in range(query_count):
            place_buf[g, pl.ds(q * own_heads, own_heads), :] = jnp.broadcast_to(
                mark_buf[g, q:q + 1, :], (own_heads, LANES)
            )

    set_places(0)
    top_buf[...] = jnp.full(top_buf.shape, first_top, jnp.float32)
    sum_buf[...] = jnp.zeros(sum_buf.shape, jnp.float32)
    acc_buf[...] = jnp.zeros(acc_buf.shape, jnp.float32)

    def await_pair(j, xx):
        for step in range(1, sub_count):
            await_block(j, xx, source_sub(step), 0, PIECES, pair_recv.at[step - 1, j, xx])

    def absorb(entries, g):
        queries = query_buf[g].reshape(rows, latent_width)
        rope_rows = rope_rows_buf[g].reshape(rows, rope_width)
        offsets = lax.broadcasted_iota(jnp.int32, (rows, LANES), 1)
        parts = []
        for j, xx, valid in entries:
            for ss in range(sub_count):
                root = (j * sect_count + xx) * sub_count + ss
                block = cache_buf[j, xx, ss, rope_rows_count:block_rows, :]
                rope_block = jnp.concatenate([
                    cache_buf[j, xx, ss, 0:rope_rows_count, i * token_count:(i + 1) * token_count] for i in range(folds)
                ], axis=0)
                scores = lax.dot_general(
                    queries, block, (((1,), (1,)), ((), ())), preferred_element_type=jnp.float32,
                )
                scores = (scores + jnp.dot(rope_rows, rope_block, preferred_element_type=jnp.float32)) * score_scale
                length = length_ref[root]
                if valid is not None:
                    length = jnp.where(valid, length, 0)
                limit = jnp.minimum(length, place_buf[g] - (root * token_count - 1))
                for at in range(0, token_count, LANES):
                    parts.append(jnp.where(offsets < limit - at, scores[:, at:at + LANES], lowest_score))
        old_top = top_buf[g]
        best = functools.reduce(jnp.maximum, parts)
        new_top = jnp.maximum(old_top, jnp.max(best, axis=1, keepdims=True))
        factor = jnp.exp2(old_top - new_top)
        weights = [jnp.exp2(part - new_top) for part in parts]
        sum_buf[g] = sum_buf[g] * factor + jnp.sum(sum(weights), axis=1, keepdims=True)
        top_buf[g] = new_top
        mixed = acc_buf[g] * spread(factor, latent_width)
        per_entry = len(parts) // len(entries)
        for i, (j, xx, _) in enumerate(entries):
            block = cache_buf[j, xx, :, rope_rows_count:block_rows, :].reshape(sub_count * token_count, latent_width)
            mixed = mixed + jnp.dot(
                jnp.concatenate(
                    [part.astype(jnp.bfloat16) for part in weights[i * per_entry:(i + 1) * per_entry]], axis=1
                ),
                block, preferred_element_type=jnp.float32,
            )
        acc_buf[g] = mixed

    def inside(j):
        return (j >= 0) & (j < blk_count)

    def by_x(k, p):
        if not side or p == 0:
            return k == k
        return (k != 1) | at_end if p == 1 else k != 1

    def pass_on(k, p):
        for way in range(2):
            j = z - k if way == 0 else z + k
            target = z + 1 if way == 0 else z - 1

            @pl.when(inside(j))
            def _():
                await_block(j, x, s, p, p + 1, z_recv.at[j, p])

                @pl.when(inside(target) & ((k + 1 != last_z) if lend else (k == k)))
                def _():
                    z_copy(j, p, way, target).start()

                @pl.when(by_x(k, p))
                def _():
                    for step in range(1, sect_count):
                        x_copy(j, p, step).start()
                to_pair(j, x, p, p + 1)

    def take_sections(k, p):
        for way in range(2):
            j = z - k if way == 0 else z + k

            @pl.when(inside(j) & by_x(k, p) & ((k > 0) | (way == 0)))
            def _():
                for step in range(1, sect_count):
                    xx = source_section(step)
                    await_block(j, xx, s, p, p + 1, x_recv.at[step - 1, j, p])
                    to_pair(j, xx, p, p + 1)

    def sections(mine):
        return [x] if mine else [source_section(step) for step in range(1, sect_count)]

    def columns(k):
        return [z] if isinstance(k, int) and k == 0 else [z - k, z + k]

    def entries_at(k, mine, only=None):
        found = []
        for j in columns(k):
            valid = inside(j) if only is None else inside(j) & only
            for xx in sections(mine):
                here = jnp.where(valid, j, z)
                found.append((here, jnp.where(valid, xx, x), valid) if j is not z else (z, xx, None))
        return found

    def await_at(k, mine, only=None):
        for j in columns(k):
            @pl.when(inside(j) if only is None else inside(j) & only)
            def _():
                for xx in sections(mine):
                    await_pair(j, xx)

    def first_side(way_target):
        return (way_target == 0) | (way_target == last_z)

    def send_side():
        for way in range(2):
            target = z + 1 if way == 0 else z - 1
            for first in (1, 2):
                @pl.when(inside(target) & (first_side(target) == (first == 2)))
                def _():
                    side_copy(z, way, target, first).start()

    def take_side():
        for way in range(2):
            j = z - 1 if way == 0 else z + 1
            for first in (1, 2):
                @pl.when(inside(j) & (at_end == (first == 2)))
                def _():
                    await_block(j, other, s, first, PIECES, side_recv.at[way])
                    to_pair(j, other, first, PIECES)

    await_at(0, True)
    absorb(entries_at(0, True), 0)
    for p in range(PIECES):
        if steps > 0:
            pass_on(1, p)
        take_sections(0, p)
    if side and steps > 0:
        send_side()

    def one_step(k):
        behind = [] if side and isinstance(k, int) and k == 3 else [k - 2]
        only = (k != 3) if side and not isinstance(k, int) else None
        for p in range(PIECES):
            pass_on(k, p)
            if p == 0:
                await_at(k - 1, True)
                entries = entries_at(k - 1, True)
                for distance in behind:
                    await_at(distance, False, only)
                    entries = entries + entries_at(distance, False, only)
                absorb(entries, 0)
            else:
                take_sections(k - 1, p - 1)
        take_sections(k - 1, PIECES - 1)

    if steps <= 3:
        for k in range(2, steps + 1):
            one_step(k)
    else:
        one_step(2)

        def later_step(k, carry):
            one_step(k)
            return carry
        lax.fori_loop(3, steps + 1, later_step, 0)

    row_head = lax.rem(lax.broadcasted_iota(jnp.int32, (chunk_rows, value_width), 0), chunk_heads)

    def rows_of(value, c):
        width = value.shape[-1]
        part = value.reshape(query_count, own_heads, width)[:, c * chunk_heads:(c + 1) * chunk_heads, :]
        return part.reshape(chunk_rows, width)

    def project(g, c):
        latent = rows_of(acc_buf[g], c).astype(jnp.bfloat16)
        result = jnp.zeros((chunk_rows, value_width), jnp.float32)
        for h in range(0, chunk_heads, 2):
            pair = jnp.concatenate(
                [weight_buf[c * chunk_heads + h], weight_buf[c * chunk_heads + h + 1]], axis=1
            )
            both = jnp.dot(latent, pair, preferred_element_type=jnp.float32)
            result = jnp.where(row_head == h, both[:, :value_width], result)
            result = jnp.where(row_head == h + 1, both[:, value_width:], result)
        return result

    def take_lent():
        for copy in lend_copies:
            copy.wait_recv()
        set_places(1)
        absorb(far_mine, 0)
        absorb(far_mine, 1)

    def return_parts():
        absorb(far_others, 1)
        for c in range(chunk_count):
            part_buf[0, c] = project(1, c).astype(jnp.bfloat16)
            stat_buf[0, c, 0:8] = jnp.transpose(rows_of(top_buf[1], c))[0:8]
            stat_buf[0, c, 8:16] = jnp.transpose(rows_of(sum_buf[1], c))[0:8]
            for copy in part_copies(c):
                copy.start()

    if steps == 0:
        await_at(0, False)
        if sect_count > 1:
            absorb(entries_at(0, False), 0)
    else:
        far = jnp.where(z >= steps, z - steps, z + steps)
        has_far = inside(far)
        far = jnp.where(has_far, far, z)
        far_mine = [(far, x, has_far)]
        far_others = [(far, jnp.where(has_far, xx, x), has_far) for xx in sections(False)]
        await_at(steps, True)
        if lend:
            pl.when(helper)(take_lent)

            @pl.when(jnp.logical_not(helper))
            def _():
                absorb(far_mine, 0)
        else:
            absorb(far_mine, 0)
        for p in range(PIECES):
            take_sections(steps, p)
        if side:
            take_side()
        weight_copy.wait()
        await_at(steps, False)
        if lend:
            pl.when(helper)(return_parts)
        left = sorted({steps - 1} | ({1} if side and steps > 1 else set()))
        rest = list(far_others)
        for k in left:
            await_at(k, False)
            rest = rest + entries_at(k, False)
        if rest:
            absorb(rest, 0)

    def drain(j, carry):
        def whole_wait(xx, sem):
            block_send(j, xx, 0, PIECES, sem, sem, {"sub": s}).wait_send()

        far_up = ((j == 0) & (z + 1 == last_z)) if lend else (j < 0)
        far_down = ((j == last_z) & (z == 1)) if lend else (j < 0)
        here = ((j - z != last_z) & (z - j != last_z)) if lend else (j >= 0)

        @pl.when((j <= z) & (z < last_z) & jnp.logical_not(far_up))
        def _():
            whole_wait(x, z_send.at[0, j])

        @pl.when((j >= z) & (z > 0) & jnp.logical_not(far_down))
        def _():
            whole_wait(x, z_send.at[1, j])

        near = ((j == z - 1) | (j == z + 1)) if side else (j < 0)
        for step in range(1, sect_count):
            sem = x_send.at[step - 1, j]
            for end in (1, 2):
                @pl.when(near & (at_end == (end == 2)))
                def _():
                    block_send(j, x, 0, end, sem, sem, {"sub": s}).wait_send()

            @pl.when(here & jnp.logical_not(near))
            def _():
                whole_wait(x, sem)

        @pl.when(here)
        def _():
            for xx in range(sect_count):
                for step in range(1, sub_count):
                    whole_wait(xx, pair_send.at[step - 1, j, xx])
        return carry

    lax.fori_loop(0, blk_count, drain, 0)
    if side:
        for way in range(2):
            target = z + 1 if way == 0 else z - 1
            for first in (1, 2):
                @pl.when(inside(target) & (first_side(target) == (first == 2)))
                def _():
                    side_copy(z, way, z, first).wait_send()

    for c in range(chunk_count):
        result_buf[c] = project(0, c)

    def write(c, value):
        out_ref[:, c * chunk_heads:(c + 1) * chunk_heads, :] = value.reshape(
            query_count, chunk_heads, value_width
        ).astype(out_ref.dtype)

    merged = at_end if lend else (z < 0)

    @pl.when(jnp.logical_not(merged))
    def _():
        for c in range(chunk_count):
            write(c, result_buf[c] / rows_of(sum_buf[0], c))

    if lend:
        @pl.when(at_end)
        def _():
            for copy in lend_copies:
                copy.wait_send()
            for c in range(chunk_count):
                for copy in part_copies(c):
                    copy.wait_recv()
                top, total = rows_of(top_buf[0], c), rows_of(sum_buf[0], c)
                stat = stat_buf[1, c]
                far_top = jnp.transpose(jnp.broadcast_to(stat[0:1], (LANES, chunk_rows)))
                far_total = jnp.transpose(jnp.broadcast_to(stat[8:9], (LANES, chunk_rows)))
                overall = jnp.maximum(top, far_top)
                factor, far_factor = jnp.exp2(top - overall), jnp.exp2(far_top - overall)
                value = result_buf[c] * factor + part_buf[1, c].astype(jnp.float32) * far_factor
                write(c, value / (total * factor + far_total * far_factor))

        @pl.when(helper)
        def _():
            for c in range(chunk_count):
                for copy in part_copies(c):
                    copy.wait_send()


def shards(query_latent, query_rope, cache_latent, cache_rope, lengths, positions, value_weight):
    query_count, head_count, latent_width = query_latent.shape
    rope_width = query_rope.shape[1]
    token_count = cache_latent.shape[1]
    blk_count, sect_count, sub_count = (lax.axis_size(name) for name in ("blk", "sect", "sub"))
    own_heads, _, value_width = value_weight.shape
    chunk_heads = min(16, own_heads)
    chunk_count = own_heads // chunk_heads
    chunk_rows = query_count * chunk_heads
    block_rows = token_count + rope_width * token_count // latent_width
    rows = query_count * own_heads
    peers = max(sect_count - 1, 1)
    pairs = max(sub_count - 1, 1)
    bf16, f32 = jnp.bfloat16, jnp.float32
    hbm = pl.BlockSpec(memory_space=pltpu.HBM)
    vmem = pl.BlockSpec(memory_space=pltpu.VMEM)
    dma = pltpu.SemaphoreType.DMA
    return pl.pallas_call(
        functools.partial(kernel, (blk_count, sect_count, sub_count, chunk_heads)),
        out_shape=pltpu.VMEM((query_count, own_heads, value_width), bf16),
        in_specs=[hbm] * 7,
        out_specs=vmem,
        scratch_shapes=[
            pltpu.VMEM(query_rope.shape, bf16),
            pltpu.SMEM(lengths.shape, jnp.int32),
            pltpu.SMEM(positions.shape, jnp.int32),
            pltpu.VMEM((rope_width, token_count), bf16),
            pltpu.VMEM((2, query_count, own_heads, latent_width), bf16),
            pltpu.VMEM((query_count, head_count, rope_width), bf16),
            pltpu.VMEM((2, query_count, own_heads, rope_width), bf16),
            pltpu.VMEM((blk_count, sect_count, sub_count, block_rows, latent_width), bf16),
            pltpu.VMEM((own_heads, latent_width, value_width), bf16),
            pltpu.VMEM((2, query_count, LANES), jnp.int32),
            pltpu.VMEM((2, rows, LANES), jnp.int32),
            pltpu.VMEM((2, rows, LANES), f32),
            pltpu.VMEM((2, rows, LANES), f32),
            pltpu.VMEM((2, rows, latent_width), f32),
            pltpu.VMEM((chunk_count, chunk_rows, value_width), f32),
            pltpu.VMEM((2, chunk_count, chunk_rows, value_width), bf16),
            pltpu.VMEM((2, chunk_count, 16, chunk_rows), f32),
            dma((7,)),
            dma((2, blk_count)),
            dma((blk_count, PIECES)),
            dma((peers, blk_count)),
            dma((peers, blk_count, PIECES)),
            dma((pairs, blk_count, sect_count)),
            dma((pairs, blk_count, sect_count)),
            dma((2,)),
            dma((2,)),
            dma((3,)),
            dma((3,)),
            dma((chunk_count, 2)),
            dma((chunk_count, 2)),
        ],
        compiler_params=pltpu.CompilerParams(
            collective_id=0, has_side_effects=True, vmem_limit_bytes=60 * 1024 * 1024
        ),
    )(query_latent, query_rope, cache_latent, cache_rope, lengths, positions, value_weight)


def solution(mesh):
    placed = (
        P(("rep", "blk"), None, None),
        P(("rep", "blk"), None, None),
        P(("rep", "blk", "sect", "sub"), None, None),
        P(("rep", "blk", "sect", "sub"), None, None),
        P("rep"),
        P(("rep", "blk")),
        P(("sect", "sub"), None, None),
    )
    return jax.shard_map(
        shards,
        mesh=mesh,
        in_specs=placed,
        out_specs=P(("rep", "blk"), ("sect", "sub"), None),
        check_vma=False,
    )
```

```python
import functools
import math

import jax
import jax.numpy as jnp
from jax import lax
from jax.experimental import pallas as pl
from jax.experimental.pallas import tpu as pltpu
from jax.sharding import PartitionSpec as P

lowest_score = -1e30
first_top = -1e29
LANES = 128
PIECES = 3
MESH = pl.DeviceIdType.MESH


def spread(column, width):
    return jnp.concatenate([column] * (width // LANES), axis=1)


def kernel(
    sizes, query_hbm, rope_q_hbm, latent_hbm, rope_hbm, length_hbm, position_hbm, weight_hbm,
    out_ref,
    rope_q_ref, length_ref, position_ref, rope_stage, query_buf, rope_q_buf, rope_rows_buf, cache_buf, weight_buf,
    mark_buf, place_buf, top_buf, sum_buf, acc_buf, result_buf, part_buf, stat_buf,
    local_sem, z_send, z_recv, x_send, x_recv, pair_send, pair_recv, side_send, side_recv,
    lend_send, lend_recv, part_send, part_recv,
):
    blk_count, sect_count, sub_count, chunk_heads = sizes
    _, query_count, own_heads, latent_width = query_buf.shape
    rope_width = rope_q_hbm.shape[1]
    token_count = latent_hbm.shape[1]
    value_width = weight_hbm.shape[2]
    folds = latent_width // token_count
    rope_rows_count = rope_width // folds
    block_rows = rope_rows_count + token_count
    bounds = [i * block_rows // PIECES for i in range(PIECES + 1)]
    rows = query_count * own_heads
    chunk_count = own_heads // chunk_heads
    chunk_rows = query_count * chunk_heads
    score_scale = math.log2(math.e) / math.sqrt(latent_width + rope_width)
    z = lax.axis_index("blk")
    x = lax.axis_index("sect")
    s = lax.axis_index("sub")
    last_z = blk_count - 1
    other = lax.rem(x + 1, sect_count)
    at_end = (z == 0) | (z == last_z)
    side = sect_count == 2
    lend = blk_count >= 4
    steps = last_z - 1 if lend else last_z
    helper = ((z == 1) | (z == last_z - 1)) if lend else (z < 0)

    barrier = pltpu.get_barrier_semaphore()

    def greet(device_id):
        pl.semaphore_signal(barrier, inc=1, device_id=device_id, device_id_type=MESH)

    for step in range(1, sub_count):
        greet({"sub": lax.rem(s + step, sub_count)})
    for step in range(1, sect_count):
        greet({"sect": lax.rem(x + step, sect_count)})

    @pl.when(z > 0)
    def _():
        greet({"blk": z - 1})

    @pl.when(z < last_z)
    def _():
        greet({"blk": z + 1})

    heads_at = pl.multiple_of((x * sub_count + s) * own_heads, own_heads)
    own_copies = [
        pltpu.make_async_copy(
            latent_hbm.at[0], cache_buf.at[z, x, s, pl.ds(rope_rows_count, token_count)], local_sem.at[0]
        ),
        pltpu.make_async_copy(rope_hbm.at[0], rope_stage, local_sem.at[1]),
    ]
    small_copies = [
        pltpu.make_async_copy(source, landing, local_sem.at[2 + i])
        for i, (source, landing) in enumerate((
            (rope_q_hbm, rope_q_ref), (length_hbm, length_ref), (position_hbm, position_ref),
            (query_hbm.at[:, pl.ds(heads_at, own_heads), :], query_buf.at[0]),
        ))
    ]
    weight_copy = pltpu.make_async_copy(weight_hbm, weight_buf, local_sem.at[0])
    for copy in own_copies + small_copies:
        copy.start()

    def send(source, landing, send_sem, recv_sem, device_id):
        return pltpu.make_async_remote_copy(
            src_ref=source, dst_ref=landing, send_sem=send_sem, recv_sem=recv_sem,
            device_id=device_id, device_id_type=MESH,
        )

    def place(j, xx, ss, first, end):
        return cache_buf.at[j, xx, ss, pl.ds(bounds[first], bounds[end] - bounds[first])]

    def block_send(j, xx, first, end, send_sem, recv_sem, device_id):
        here = place(j, xx, s, first, end)
        return send(here, here, send_sem, recv_sem, device_id)

    def await_block(j, xx, ss, first, end, recv_sem):
        here = place(j, xx, ss, first, end)
        send(here, here, recv_sem, recv_sem, {"sub": s}).wait_recv()

    def z_copy(j, p, way, target):
        away = z - j if way == 0 else j - z
        return block_send(j, x, p, p + 1, z_send.at[way, away], z_recv.at[j, p], {"blk": target})

    def x_copy(j, p, step):
        return block_send(
            j, x, p, p + 1, x_send.at[step - 1, j], x_recv.at[step - 1, j, p],
            {"sect": lax.rem(x + step, sect_count)},
        )

    def source_section(step):
        return lax.rem(x + sect_count - step, sect_count)

    def source_sub(step):
        return lax.rem(s + sub_count - step, sub_count)

    def to_pair(j, xx, first, end):
        for step in range(1, sub_count):
            block_send(
                j, xx, first, end, pair_send.at[step - 1, j], pair_recv.at[step - 1, j, xx],
                {"sub": lax.rem(s + step, sub_count)},
            ).start()

    def side_copy(j, way, target, first):
        return block_send(j, other, first, PIECES, side_send.at[way], side_recv.at[way], {"blk": target})

    inward = jnp.where(z == 0, 1, last_z - 1)
    outward = jnp.where(z == 1, 0, last_z)
    lend_copies = [
        send(ref.at[0], ref.at[1], lend_send.at[i], lend_recv.at[i], {"blk": inward})
        for i, ref in enumerate((query_buf, rope_rows_buf, mark_buf))
    ]

    def part_copies(c):
        return [
            send(ref.at[0, c], ref.at[1, c], part_send.at[i], part_recv.at[c, i], {"blk": outward})
            for i, ref in enumerate((part_buf, stat_buf))
        ]

    neighbours = jnp.where(z > 0, 1, 0) + jnp.where(z < last_z, 1, 0)
    for copy in own_copies:
        copy.wait()
    for i in range(folds):
        cache_buf[z, x, s, 0:rope_rows_count, i * token_count:(i + 1) * token_count] = (
            rope_stage[i * rope_rows_count:(i + 1) * rope_rows_count, :]
        )
    pl.semaphore_wait(barrier, sub_count - 1 + sect_count - 1 + neighbours)

    for p in range(PIECES):
        @pl.when(z < last_z)
        def _():
            z_copy(z, p, 0, z + 1).start()

        @pl.when(z > 0)
        def _():
            z_copy(z, p, 1, z - 1).start()

        for step in range(1, sect_count):
            x_copy(z, p, step).start()
        to_pair(z, x, p, p + 1)

    for copy in small_copies:
        copy.wait()
    for q in range(query_count):
        rope_q_buf[q] = jnp.transpose(rope_q_ref[q].astype(jnp.float32)).astype(jnp.bfloat16)
        mark_buf[0, q:q + 1, :] = jnp.full((1, LANES), position_ref[q], jnp.int32)
    rope_rows_buf[0] = rope_q_buf[:, pl.ds(heads_at, own_heads), :]
    if lend:
        @pl.when(at_end)
        def _():
            for copy in lend_copies:
                copy.start()
    weight_copy.start()

    def set_places(g):
        for q in range(query_count):
            place_buf[g, pl.ds(q * own_heads, own_heads), :] = jnp.broadcast_to(
                mark_buf[g, q:q + 1, :], (own_heads, LANES)
            )

    set_places(0)
    top_buf[...] = jnp.full(top_buf.shape, first_top, jnp.float32)
    sum_buf[...] = jnp.zeros(sum_buf.shape, jnp.float32)
    acc_buf[...] = jnp.zeros(acc_buf.shape, jnp.float32)

    def await_pair(j, xx):
        for step in range(1, sub_count):
            await_block(j, xx, source_sub(step), 0, PIECES, pair_recv.at[step - 1, j, xx])

    def absorb(entries, g):
        queries = query_buf[g].reshape(rows, latent_width)
        rope_rows = rope_rows_buf[g].reshape(rows, rope_width)
        offsets = lax.broadcasted_iota(jnp.int32, (rows, LANES), 1)
        parts = []
        for j, xx, valid in entries:
            for ss in range(sub_count):
                root = (j * sect_count + xx) * sub_count + ss
                block = cache_buf[j, xx, ss, rope_rows_count:block_rows, :]
                rope_block = jnp.concatenate([
                    cache_buf[j, xx, ss, 0:rope_rows_count, i * token_count:(i + 1) * token_count] for i in range(folds)
                ], axis=0)
                scores = lax.dot_general(
                    queries, block, (((1,), (1,)), ((), ())), preferred_element_type=jnp.float32,
                )
                scores = (scores + jnp.dot(rope_rows, rope_block, preferred_element_type=jnp.float32)) * score_scale
                length = length_ref[root]
                if valid is not None:
                    length = jnp.where(valid, length, 0)
                limit = jnp.minimum(length, place_buf[g] - (root * token_count - 1))
                for at in range(0, token_count, LANES):
                    parts.append(jnp.where(offsets < limit - at, scores[:, at:at + LANES], lowest_score))
        old_top = top_buf[g]
        best = functools.reduce(jnp.maximum, parts)
        new_top = jnp.maximum(old_top, jnp.max(best, axis=1, keepdims=True))
        factor = jnp.exp2(old_top - new_top)
        weights = [jnp.exp2(part - new_top) for part in parts]
        sum_buf[g] = sum_buf[g] * factor + jnp.sum(sum(weights), axis=1, keepdims=True)
        top_buf[g] = new_top
        mixed = acc_buf[g] * spread(factor, latent_width)
        per_entry = len(parts) // len(entries)
        for i, (j, xx, _) in enumerate(entries):
            block = cache_buf[j, xx, :, rope_rows_count:block_rows, :].reshape(sub_count * token_count, latent_width)
            mixed = mixed + jnp.dot(
                jnp.concatenate(
                    [part.astype(jnp.bfloat16) for part in weights[i * per_entry:(i + 1) * per_entry]], axis=1
                ),
                block, preferred_element_type=jnp.float32,
            )
        acc_buf[g] = mixed

    def inside(j):
        return (j >= 0) & (j < blk_count)

    def by_x(k, p):
        if not side or p == 0:
            return k == k
        return (k != 1) | at_end if p == 1 else k != 1

    def pass_on(k, p):
        for way in range(2):
            j = z - k if way == 0 else z + k
            target = z + 1 if way == 0 else z - 1

            @pl.when(inside(j))
            def _():
                await_block(j, x, s, p, p + 1, z_recv.at[j, p])

                @pl.when(inside(target) & ((k + 1 != last_z) if lend else (k == k)))
                def _():
                    z_copy(j, p, way, target).start()

                @pl.when(by_x(k, p))
                def _():
                    for step in range(1, sect_count):
                        x_copy(j, p, step).start()
                to_pair(j, x, p, p + 1)

    def take_sections(k, p):
        for way in range(2):
            j = z - k if way == 0 else z + k

            @pl.when(inside(j) & by_x(k, p) & ((k > 0) | (way == 0)))
            def _():
                for step in range(1, sect_count):
                    xx = source_section(step)
                    await_block(j, xx, s, p, p + 1, x_recv.at[step - 1, j, p])
                    to_pair(j, xx, p, p + 1)

    def sections(mine):
        return [x] if mine else [source_section(step) for step in range(1, sect_count)]

    def columns(k):
        return [z] if isinstance(k, int) and k == 0 else [z - k, z + k]

    def entries_at(k, mine, only=None):
        found = []
        for j in columns(k):
            valid = inside(j) if only is None else inside(j) & only
            for xx in sections(mine):
                here = jnp.where(valid, j, z)
                found.append((here, jnp.where(valid, xx, x), valid) if j is not z else (z, xx, None))
        return found

    def await_at(k, mine, only=None):
        for j in columns(k):
            @pl.when(inside(j) if only is None else inside(j) & only)
            def _():
                for xx in sections(mine):
                    await_pair(j, xx)

    def first_side(way_target):
        return (way_target == 0) | (way_target == last_z)

    def send_side():
        for way in range(2):
            target = z + 1 if way == 0 else z - 1
            for first in (1, 2):
                @pl.when(inside(target) & (first_side(target) == (first == 2)))
                def _():
                    side_copy(z, way, target, first).start()

    def take_side():
        for way in range(2):
            j = z - 1 if way == 0 else z + 1
            for first in (1, 2):
                @pl.when(inside(j) & (at_end == (first == 2)))
                def _():
                    await_block(j, other, s, first, PIECES, side_recv.at[way])
                    to_pair(j, other, first, PIECES)

    await_at(0, True)
    absorb(entries_at(0, True), 0)
    for p in range(PIECES):
        if steps > 0:
            pass_on(1, p)
        take_sections(0, p)
    if side and steps > 0:
        send_side()

    def one_step(k):
        behind = [] if side and isinstance(k, int) and k == 3 else [k - 2]
        only = (k != 3) if side and not isinstance(k, int) else None
        for p in range(PIECES):
            pass_on(k, p)
            if p == 0:
                await_at(k - 1, True)
                entries = entries_at(k - 1, True)
                for distance in behind:
                    await_at(distance, False, only)
                    entries = entries + entries_at(distance, False, only)
                absorb(entries, 0)
            else:
                take_sections(k - 1, p - 1)
        take_sections(k - 1, PIECES - 1)

    if steps <= 3:
        for k in range(2, steps + 1):
            one_step(k)
    else:
        one_step(2)

        def later_step(k, carry):
            one_step(k)
            return carry
        lax.fori_loop(3, steps + 1, later_step, 0)

    row_head = lax.rem(lax.broadcasted_iota(jnp.int32, (chunk_rows, value_width), 0), chunk_heads)

    def rows_of(value, c):
        width = value.shape[-1]
        part = value.reshape(query_count, own_heads, width)[:, c * chunk_heads:(c + 1) * chunk_heads, :]
        return part.reshape(chunk_rows, width)

    def project(g, c):
        latent = rows_of(acc_buf[g], c).astype(jnp.bfloat16)
        result = jnp.zeros((chunk_rows, value_width), jnp.float32)
        for h in range(0, chunk_heads, 2):
            pair = jnp.concatenate(
                [weight_buf[c * chunk_heads + h], weight_buf[c * chunk_heads + h + 1]], axis=1
            )
            both = jnp.dot(latent, pair, preferred_element_type=jnp.float32)
            result = jnp.where(row_head == h, both[:, :value_width], result)
            result = jnp.where(row_head == h + 1, both[:, value_width:], result)
        return result

    def take_lent():
        for copy in lend_copies:
            copy.wait_recv()
        set_places(1)
        absorb(far_mine, 0)
        absorb(far_mine, 1)

    def return_parts():
        absorb(far_others, 1)
        for c in range(chunk_count):
            part_buf[0, c] = project(1, c).astype(jnp.bfloat16)
            tops, totals = (jnp.transpose(rows_of(ref[1], c))[0:8] for ref in (top_buf, sum_buf))
            stat_buf[0, c] = jnp.where(lax.broadcasted_iota(jnp.int32, tops.shape, 0) == 0, tops, totals)
            for copy in part_copies(c):
                copy.start()

    if steps == 0:
        await_at(0, False)
        if sect_count > 1:
            absorb(entries_at(0, False), 0)
    else:
        far = jnp.where(z >= steps, z - steps, z + steps)
        has_far = inside(far)
        far = jnp.where(has_far, far, z)
        far_mine = [(far, x, has_far)]
        far_others = [(far, jnp.where(has_far, xx, x), has_far) for xx in sections(False)]
        await_at(steps, True)
        if lend:
            pl.when(helper)(take_lent)

            @pl.when(jnp.logical_not(helper))
            def _():
                absorb(far_mine, 0)
        else:
            absorb(far_mine, 0)
        for p in range(PIECES):
            take_sections(steps, p)
        if side:
            take_side()
        weight_copy.wait()
        await_at(steps, False)
        if lend:
            pl.when(helper)(return_parts)
        left = sorted({steps - 1} | ({1} if side and steps > 1 else set()))
        rest = list(far_others)
        for k in left:
            await_at(k, False)
            rest = rest + entries_at(k, False)
        if rest:
            absorb(rest, 0)

    def drain(j, carry):
        def whole_wait(xx, sem):
            block_send(j, xx, 0, PIECES, sem, sem, {"sub": s}).wait_send()

        far_up = ((j == 0) & (z + 1 == last_z)) if lend else (j < 0)
        far_down = ((j == last_z) & (z == 1)) if lend else (j < 0)
        here = ((j - z != last_z) & (z - j != last_z)) if lend else (j >= 0)

        @pl.when((j <= z) & (z < last_z) & jnp.logical_not(far_up))
        def _():
            whole_wait(x, z_send.at[0, z - j])

        @pl.when((j >= z) & (z > 0) & jnp.logical_not(far_down))
        def _():
            whole_wait(x, z_send.at[1, j - z])

        near = ((j == z - 1) | (j == z + 1)) if side else (j < 0)
        for step in range(1, sect_count):
            sem = x_send.at[step - 1, j]
            for end in (1, 2):
                @pl.when(near & (at_end == (end == 2)))
                def _():
                    block_send(j, x, 0, end, sem, sem, {"sub": s}).wait_send()

            @pl.when(here & jnp.logical_not(near))
            def _():
                whole_wait(x, sem)

        @pl.when(here)
        def _():
            for step in range(1, sub_count):
                all_sections, sem = cache_buf.at[j, :, s], pair_send.at[step - 1, j]
                send(all_sections, all_sections, sem, sem, {"sub": s}).wait_send()
        return carry

    lax.fori_loop(0, blk_count, drain, 0)
    if side:
        for way in range(2):
            target = z + 1 if way == 0 else z - 1
            for first in (1, 2):
                @pl.when(inside(target) & (first_side(target) == (first == 2)))
                def _():
                    side_copy(z, way, z, first).wait_send()

    for c in range(chunk_count):
        result_buf[c] = project(0, c)

    def write(c, value):
        out_ref[:, c * chunk_heads:(c + 1) * chunk_heads, :] = value.reshape(
            query_count, chunk_heads, value_width
        ).astype(out_ref.dtype)

    merged = at_end if lend else (z < 0)

    @pl.when(jnp.logical_not(merged))
    def _():
        for c in range(chunk_count):
            write(c, result_buf[c] / rows_of(sum_buf[0], c))

    if lend:
        @pl.when(at_end)
        def _():
            for copy in lend_copies:
                copy.wait_send()
            for c in range(chunk_count):
                for copy in part_copies(c):
                    copy.wait_recv()
                top, total = rows_of(top_buf[0], c), rows_of(sum_buf[0], c)
                stat = stat_buf[1, c]
                far_top = jnp.transpose(jnp.broadcast_to(stat[0:1], (LANES, chunk_rows)))
                far_total = jnp.transpose(jnp.broadcast_to(stat[1:2], (LANES, chunk_rows)))
                overall = jnp.maximum(top, far_top)
                factor, far_factor = jnp.exp2(top - overall), jnp.exp2(far_top - overall)
                value = result_buf[c] * factor + part_buf[1, c].astype(jnp.float32) * far_factor
                write(c, value / (total * factor + far_total * far_factor))

        @pl.when(helper)
        def _():
            for i, ref in enumerate((part_buf, stat_buf)):
                send(ref.at[0], ref.at[1], part_send.at[i], part_send.at[i], {"blk": outward}).wait_send()


def shards(query_latent, query_rope, cache_latent, cache_rope, lengths, positions, value_weight):
    query_count, head_count, latent_width = query_latent.shape
    rope_width = query_rope.shape[1]
    token_count = cache_latent.shape[1]
    blk_count, sect_count, sub_count = (lax.axis_size(name) for name in ("blk", "sect", "sub"))
    own_heads, _, value_width = value_weight.shape
    chunk_heads = min(16, own_heads)
    chunk_count = own_heads // chunk_heads
    chunk_rows = query_count * chunk_heads
    block_rows = token_count + rope_width * token_count // latent_width
    rows = query_count * own_heads
    peers = max(sect_count - 1, 1)
    pairs = max(sub_count - 1, 1)
    bf16, f32 = jnp.bfloat16, jnp.float32
    hbm = pl.BlockSpec(memory_space=pltpu.HBM)
    vmem = pl.BlockSpec(memory_space=pltpu.VMEM)
    dma = pltpu.SemaphoreType.DMA
    return pl.pallas_call(
        functools.partial(kernel, (blk_count, sect_count, sub_count, chunk_heads)),
        out_shape=pltpu.VMEM((query_count, own_heads, value_width), bf16),
        in_specs=[hbm] * 7,
        out_specs=vmem,
        scratch_shapes=[
            pltpu.VMEM(query_rope.shape, bf16),
            pltpu.SMEM(lengths.shape, jnp.int32),
            pltpu.SMEM(positions.shape, jnp.int32),
            pltpu.VMEM((rope_width, token_count), bf16),
            pltpu.VMEM((2, query_count, own_heads, latent_width), bf16),
            pltpu.VMEM((query_count, head_count, rope_width), bf16),
            pltpu.VMEM((2, query_count, own_heads, rope_width), bf16),
            pltpu.VMEM((blk_count, sect_count, sub_count, block_rows, latent_width), bf16),
            pltpu.VMEM((own_heads, latent_width, value_width), bf16),
            pltpu.VMEM((2, query_count, LANES), jnp.int32),
            pltpu.VMEM((2, rows, LANES), jnp.int32),
            pltpu.VMEM((2, rows, LANES), f32),
            pltpu.VMEM((2, rows, LANES), f32),
            pltpu.VMEM((2, rows, latent_width), f32),
            pltpu.VMEM((chunk_count, chunk_rows, value_width), f32),
            pltpu.VMEM((2, chunk_count, chunk_rows, value_width), bf16),
            pltpu.VMEM((2, chunk_count, 8, chunk_rows), f32),
            dma((6,)),
            dma((2, max(blk_count - 1, 1))),
            dma((blk_count, PIECES)),
            dma((peers, blk_count)),
            dma((peers, blk_count, PIECES)),
            dma((pairs, blk_count)),
            dma((pairs, blk_count, sect_count)),
            dma((2,)),
            dma((2,)),
            dma((3,)),
            dma((3,)),
            dma((2,)),
            dma((chunk_count, 2)),
        ],
        compiler_params=pltpu.CompilerParams(
            collective_id=0, has_side_effects=True, vmem_limit_bytes=60 * 1024 * 1024
        ),
    )(query_latent, query_rope, cache_latent, cache_rope, lengths, positions, value_weight)


def solution(mesh):
    placed = (
        P(("rep", "blk"), None, None),
        P(("rep", "blk"), None, None),
        P(("rep", "blk", "sect", "sub"), None, None),
        P(("rep", "blk", "sect", "sub"), None, None),
        P("rep"),
        P(("rep", "blk")),
        P(("sect", "sub"), None, None),
    )
    return jax.shard_map(
        shards,
        mesh=mesh,
        in_specs=placed,
        out_specs=P(("rep", "blk"), ("sect", "sub"), None),
        check_vma=False,
    )
```

```python
import functools
import math

import jax
import jax.numpy as jnp
from jax import lax
from jax.experimental import pallas as pl
from jax.experimental.pallas import tpu as pltpu
from jax.sharding import PartitionSpec as P

lowest_score = -1e30
first_top = -1e29
LANES = 128
PIECES = 3
MESH = pl.DeviceIdType.MESH


def spread(column, width):
    return jnp.concatenate([column] * (width // LANES), axis=1)


def kernel(
    sizes, query_hbm, rope_q_hbm, latent_hbm, rope_hbm, length_hbm, position_hbm, weight_hbm,
    out_ref,
    rope_q_ref, length_ref, position_ref, rope_stage, query_buf, rope_q_buf, rope_rows_buf, cache_buf, weight_buf,
    mark_buf, place_buf, top_buf, sum_buf, acc_buf, result_buf, part_buf, stat_buf,
    local_sem, z_send, z_recv, x_send, x_recv, pair_send, pair_recv, side_send, side_recv,
    lend_send, lend_recv, part_send, part_recv,
):
    blk_count, sect_count, sub_count, chunk_heads = sizes
    _, query_count, own_heads, latent_width = query_buf.shape
    rope_width = rope_q_hbm.shape[1]
    token_count = latent_hbm.shape[1]
    value_width = weight_hbm.shape[2]
    folds = latent_width // token_count
    rope_rows_count = rope_width // folds
    block_rows = rope_rows_count + token_count
    bounds = [i * block_rows // PIECES for i in range(PIECES + 1)]
    rows = query_count * own_heads
    chunk_count = own_heads // chunk_heads
    chunk_rows = query_count * chunk_heads
    score_scale = math.log2(math.e) / math.sqrt(latent_width + rope_width)
    z = lax.axis_index("blk")
    x = lax.axis_index("sect")
    s = lax.axis_index("sub")
    last_z = blk_count - 1
    other = lax.rem(x + 1, sect_count)
    at_end = (z == 0) | (z == last_z)
    side = sect_count == 2
    lend = blk_count >= 4
    steps = last_z - 1 if lend else last_z
    helper = ((z == 1) | (z == last_z - 1)) if lend else (z < 0)

    barrier = pltpu.get_barrier_semaphore()

    def greet(device_id):
        pl.semaphore_signal(barrier, inc=1, device_id=device_id, device_id_type=MESH)

    for step in range(1, sub_count):
        greet({"sub": lax.rem(s + step, sub_count)})
    for step in range(1, sect_count):
        greet({"sect": lax.rem(x + step, sect_count)})

    @pl.when(z > 0)
    def _():
        greet({"blk": z - 1})

    @pl.when(z < last_z)
    def _():
        greet({"blk": z + 1})

    heads_at = pl.multiple_of((x * sub_count + s) * own_heads, own_heads)
    own_copies = [
        pltpu.make_async_copy(
            latent_hbm.at[0], cache_buf.at[z, x, s, pl.ds(rope_rows_count, token_count)], local_sem.at[0]
        ),
        pltpu.make_async_copy(rope_hbm.at[0], rope_stage, local_sem.at[1]),
    ]
    small_copies = [
        pltpu.make_async_copy(source, landing, local_sem.at[2 + i])
        for i, (source, landing) in enumerate((
            (rope_q_hbm, rope_q_ref), (length_hbm, length_ref), (position_hbm, position_ref),
            (query_hbm.at[:, pl.ds(heads_at, own_heads), :], query_buf.at[0]),
        ))
    ]
    weight_copy = pltpu.make_async_copy(weight_hbm, weight_buf, local_sem.at[0])
    for copy in own_copies + small_copies:
        copy.start()

    def send(source, landing, send_sem, recv_sem, device_id):
        return pltpu.make_async_remote_copy(
            src_ref=source, dst_ref=landing, send_sem=send_sem, recv_sem=recv_sem,
            device_id=device_id, device_id_type=MESH,
        )

    def place(j, xx, ss, first, end):
        return cache_buf.at[j, xx, ss, pl.ds(bounds[first], bounds[end] - bounds[first])]

    def block_send(j, xx, first, end, send_sem, recv_sem, device_id):
        here = place(j, xx, s, first, end)
        return send(here, here, send_sem, recv_sem, device_id)

    def await_block(j, xx, ss, first, end, recv_sem):
        here = place(j, xx, ss, first, end)
        send(here, here, recv_sem, recv_sem, {"sub": s}).wait_recv()

    def z_copy(j, p, way, target):
        away = z - j if way == 0 else j - z
        return block_send(j, x, p, p + 1, z_send.at[way, away], z_recv.at[j, p], {"blk": target})

    def x_copy(j, p, step):
        return block_send(
            j, x, p, p + 1, x_send.at[step - 1, j], x_recv.at[step - 1, j, p],
            {"sect": lax.rem(x + step, sect_count)},
        )

    def source_section(step):
        return lax.rem(x + sect_count - step, sect_count)

    def source_sub(step):
        return lax.rem(s + sub_count - step, sub_count)

    def to_pair(j, xx, first, end):
        for step in range(1, sub_count):
            block_send(
                j, xx, first, end, pair_send.at[step - 1, j], pair_recv.at[step - 1, j, xx],
                {"sub": lax.rem(s + step, sub_count)},
            ).start()

    def side_copy(j, way, target, first):
        return block_send(j, other, first, PIECES, side_send.at[way], side_recv.at[way], {"blk": target})

    inward = jnp.where(z == 0, 1, last_z - 1)
    outward = jnp.where(z == 1, 0, last_z)
    lend_copies = [
        send(ref.at[0], ref.at[1], lend_send.at[i], lend_recv.at[i], {"blk": inward})
        for i, ref in enumerate((query_buf, rope_rows_buf, mark_buf))
    ]

    def part_copy(c, i):
        ref = (part_buf, stat_buf)[i]
        return send(ref.at[0, c], ref.at[1, c], part_send.at[i], part_recv.at[c, i], {"blk": outward})

    neighbours = jnp.where(z > 0, 1, 0) + jnp.where(z < last_z, 1, 0)
    for copy in own_copies:
        copy.wait()
    for i in range(folds):
        cache_buf[z, x, s, 0:rope_rows_count, i * token_count:(i + 1) * token_count] = (
            rope_stage[i * rope_rows_count:(i + 1) * rope_rows_count, :]
        )
    pl.semaphore_wait(barrier, sub_count - 1 + sect_count - 1 + neighbours)

    for p in range(PIECES):
        @pl.when(z < last_z)
        def _():
            z_copy(z, p, 0, z + 1).start()

        @pl.when(z > 0)
        def _():
            z_copy(z, p, 1, z - 1).start()

        for step in range(1, sect_count):
            x_copy(z, p, step).start()
        to_pair(z, x, p, p + 1)

    for copy in small_copies:
        copy.wait()
    for q in range(query_count):
        rope_q_buf[q] = jnp.transpose(rope_q_ref[q].astype(jnp.float32)).astype(jnp.bfloat16)
        mark_buf[0, q:q + 1, :] = jnp.full((1, LANES), position_ref[q], jnp.int32)
    rope_rows_buf[0] = rope_q_buf[:, pl.ds(heads_at, own_heads), :]
    if lend:
        @pl.when(at_end)
        def _():
            for copy in lend_copies:
                copy.start()
    weight_copy.start()

    def set_places(g):
        for q in range(query_count):
            place_buf[g, pl.ds(q * own_heads, own_heads), :] = jnp.broadcast_to(
                mark_buf[g, q:q + 1, :], (own_heads, LANES)
            )

    set_places(0)
    top_buf[...] = jnp.full(top_buf.shape, first_top, jnp.float32)
    sum_buf[...] = jnp.zeros(sum_buf.shape, jnp.float32)
    acc_buf[...] = jnp.zeros(acc_buf.shape, jnp.float32)

    def await_pair(j, xx):
        for step in range(1, sub_count):
            await_block(j, xx, source_sub(step), 0, PIECES, pair_recv.at[step - 1, j, xx])

    def absorb(entries, g):
        queries = query_buf[g].reshape(rows, latent_width)
        rope_rows = rope_rows_buf[g].reshape(rows, rope_width)
        offsets = lax.broadcasted_iota(jnp.int32, (rows, LANES), 1)
        parts = []
        for j, xx, valid in entries:
            for ss in range(sub_count):
                root = (j * sect_count + xx) * sub_count + ss
                block = cache_buf[j, xx, ss, rope_rows_count:block_rows, :]
                rope_block = jnp.concatenate([
                    cache_buf[j, xx, ss, 0:rope_rows_count, i * token_count:(i + 1) * token_count] for i in range(folds)
                ], axis=0)
                scores = lax.dot_general(
                    queries, block, (((1,), (1,)), ((), ())), preferred_element_type=jnp.float32,
                )
                scores = (scores + jnp.dot(rope_rows, rope_block, preferred_element_type=jnp.float32)) * score_scale
                length = length_ref[root]
                if valid is not None:
                    length = jnp.where(valid, length, 0)
                limit = jnp.minimum(length, place_buf[g] - (root * token_count - 1))
                for at in range(0, token_count, LANES):
                    parts.append(jnp.where(offsets < limit - at, scores[:, at:at + LANES], lowest_score))
        old_top = top_buf[g]
        best = functools.reduce(jnp.maximum, parts)
        new_top = jnp.maximum(old_top, jnp.max(best, axis=1, keepdims=True))
        factor = jnp.exp2(old_top - new_top)
        weights = [jnp.exp2(part - new_top) for part in parts]
        sum_buf[g] = sum_buf[g] * factor + jnp.sum(sum(weights), axis=1, keepdims=True)
        top_buf[g] = new_top
        mixed = acc_buf[g] * spread(factor, latent_width)
        per_entry = len(parts) // len(entries)
        for i, (j, xx, _) in enumerate(entries):
            block = cache_buf[j, xx, :, rope_rows_count:block_rows, :].reshape(sub_count * token_count, latent_width)
            mixed = mixed + jnp.dot(
                jnp.concatenate(
                    [part.astype(jnp.bfloat16) for part in weights[i * per_entry:(i + 1) * per_entry]], axis=1
                ),
                block, preferred_element_type=jnp.float32,
            )
        acc_buf[g] = mixed

    def inside(j):
        return (j >= 0) & (j < blk_count)

    def by_x(k, p):
        if not side or p == 0:
            return k == k
        return (k != 1) | at_end if p == 1 else k != 1

    def pass_on(k, p):
        for way in range(2):
            j = z - k if way == 0 else z + k
            target = z + 1 if way == 0 else z - 1

            @pl.when(inside(j))
            def _():
                await_block(j, x, s, p, p + 1, z_recv.at[j, p])

                @pl.when(inside(target) & ((k + 1 != last_z) if lend else (k == k)))
                def _():
                    z_copy(j, p, way, target).start()

                @pl.when(by_x(k, p))
                def _():
                    for step in range(1, sect_count):
                        x_copy(j, p, step).start()
                to_pair(j, x, p, p + 1)

    def take_sections(k, p):
        for way in range(2):
            j = z - k if way == 0 else z + k

            @pl.when(inside(j) & by_x(k, p) & ((k > 0) | (way == 0)))
            def _():
                for step in range(1, sect_count):
                    xx = source_section(step)
                    await_block(j, xx, s, p, p + 1, x_recv.at[step - 1, j, p])
                    to_pair(j, xx, p, p + 1)

    def sections(mine):
        return [x] if mine else [source_section(step) for step in range(1, sect_count)]

    def columns(k):
        return [z] if isinstance(k, int) and k == 0 else [z - k, z + k]

    def entries_at(k, mine, only=None):
        found = []
        for j in columns(k):
            valid = inside(j) if only is None else inside(j) & only
            for xx in sections(mine):
                here = jnp.where(valid, j, z)
                found.append((here, jnp.where(valid, xx, x), valid) if j is not z else (z, xx, None))
        return found

    def await_at(k, mine, only=None):
        for j in columns(k):
            @pl.when(inside(j) if only is None else inside(j) & only)
            def _():
                for xx in sections(mine):
                    await_pair(j, xx)

    def first_side(way_target):
        return (way_target == 0) | (way_target == last_z)

    def send_side():
        for way in range(2):
            target = z + 1 if way == 0 else z - 1
            for first in (1, 2):
                @pl.when(inside(target) & (first_side(target) == (first == 2)))
                def _():
                    side_copy(z, way, target, first).start()

    def take_side():
        for way in range(2):
            j = z - 1 if way == 0 else z + 1
            for first in (1, 2):
                @pl.when(inside(j) & (at_end == (first == 2)))
                def _():
                    await_block(j, other, s, first, PIECES, side_recv.at[way])
                    to_pair(j, other, first, PIECES)

    await_at(0, True)
    absorb(entries_at(0, True), 0)
    for p in range(PIECES):
        if steps > 0:
            pass_on(1, p)
        take_sections(0, p)
    if side and steps > 0:
        send_side()

    def one_step(k):
        behind = [] if side and isinstance(k, int) and k == 3 else [k - 2]
        only = (k != 3) if side and not isinstance(k, int) else None
        for p in range(PIECES):
            pass_on(k, p)
            if p == 0:
                await_at(k - 1, True)
                entries = entries_at(k - 1, True)
                for distance in behind:
                    await_at(distance, False, only)
                    entries = entries + entries_at(distance, False, only)
                absorb(entries, 0)
            else:
                take_sections(k - 1, p - 1)
        take_sections(k - 1, PIECES - 1)

    if steps <= 3:
        for k in range(2, steps + 1):
            one_step(k)
    else:
        one_step(2)

        def later_step(k, carry):
            one_step(k)
            return carry
        lax.fori_loop(3, steps + 1, later_step, 0)

    row_head = lax.rem(lax.broadcasted_iota(jnp.int32, (chunk_rows, value_width), 0), chunk_heads)

    def rows_of(value, c):
        width = value.shape[-1]
        part = value.reshape(query_count, own_heads, width)[:, c * chunk_heads:(c + 1) * chunk_heads, :]
        return part.reshape(chunk_rows, width)

    def project(g, c):
        latent = rows_of(acc_buf[g], c).astype(jnp.bfloat16)
        result = jnp.zeros((chunk_rows, value_width), jnp.float32)
        for h in range(0, chunk_heads, 2):
            pair = jnp.concatenate(
                [weight_buf[c * chunk_heads + h], weight_buf[c * chunk_heads + h + 1]], axis=1
            )
            both = jnp.dot(latent, pair, preferred_element_type=jnp.float32)
            result = jnp.where(row_head == h, both[:, :value_width], result)
            result = jnp.where(row_head == h + 1, both[:, value_width:], result)
        return result

    def take_lent():
        for copy in lend_copies:
            copy.wait_recv()
        set_places(1)
        absorb(far_mine, 0)
        absorb(far_mine, 1)

    def return_parts():
        absorb(far_others, 1)
        for c in range(chunk_count):
            tops, totals = (jnp.transpose(rows_of(ref[1], c))[0:8] for ref in (top_buf, sum_buf))
            stat_buf[0, c] = jnp.where(lax.broadcasted_iota(jnp.int32, tops.shape, 0) == 0, tops, totals)
            part_copy(c, 1).start()
        for c in range(chunk_count):
            part_buf[0, c] = project(1, c).astype(jnp.bfloat16)
            part_copy(c, 0).start()

    if steps == 0:
        await_at(0, False)
        if sect_count > 1:
            absorb(entries_at(0, False), 0)
    else:
        far = jnp.where(z >= steps, z - steps, z + steps)
        has_far = inside(far)
        far = jnp.where(has_far, far, z)
        far_mine = [(far, x, has_far)]
        far_others = [(far, jnp.where(has_far, xx, x), has_far) for xx in sections(False)]
        await_at(steps, True)
        if lend:
            pl.when(helper)(take_lent)

            @pl.when(jnp.logical_not(helper))
            def _():
                absorb(far_mine, 0)
        else:
            absorb(far_mine, 0)
        for p in range(PIECES):
            take_sections(steps, p)
        if side:
            take_side()
        weight_copy.wait()
        await_at(steps, False)
        if lend:
            pl.when(helper)(return_parts)
        left = sorted({steps - 1} | ({1} if side and steps > 1 else set()))
        rest = list(far_others)
        for k in left:
            await_at(k, False)
            rest = rest + entries_at(k, False)
        if rest:
            absorb(rest, 0)

    def drain(j, carry):
        def whole_wait(xx, sem):
            block_send(j, xx, 0, PIECES, sem, sem, {"sub": s}).wait_send()

        far_up = ((j == 0) & (z + 1 == last_z)) if lend else (j < 0)
        far_down = ((j == last_z) & (z == 1)) if lend else (j < 0)
        here = ((j - z != last_z) & (z - j != last_z)) if lend else (j >= 0)

        @pl.when((j <= z) & (z < last_z) & jnp.logical_not(far_up))
        def _():
            whole_wait(x, z_send.at[0, z - j])

        @pl.when((j >= z) & (z > 0) & jnp.logical_not(far_down))
        def _():
            whole_wait(x, z_send.at[1, j - z])

        near = ((j == z - 1) | (j == z + 1)) if side else (j < 0)
        for step in range(1, sect_count):
            sem = x_send.at[step - 1, j]
            for end in (1, 2):
                @pl.when(near & (at_end == (end == 2)))
                def _():
                    block_send(j, x, 0, end, sem, sem, {"sub": s}).wait_send()

            @pl.when(here & jnp.logical_not(near))
            def _():
                whole_wait(x, sem)

        @pl.when(here)
        def _():
            for step in range(1, sub_count):
                all_sections, sem = cache_buf.at[j, :, s], pair_send.at[step - 1, j]
                send(all_sections, all_sections, sem, sem, {"sub": s}).wait_send()
        return carry

    lax.fori_loop(0, blk_count, drain, 0)
    if side:
        for way in range(2):
            target = z + 1 if way == 0 else z - 1
            for first in (1, 2):
                @pl.when(inside(target) & (first_side(target) == (first == 2)))
                def _():
                    side_copy(z, way, z, first).wait_send()

    for c in range(chunk_count):
        result_buf[c] = project(0, c)

    def write(c, value):
        out_ref[:, c * chunk_heads:(c + 1) * chunk_heads, :] = value.reshape(
            query_count, chunk_heads, value_width
        ).astype(out_ref.dtype)

    merged = at_end if lend else (z < 0)

    @pl.when(jnp.logical_not(merged))
    def _():
        for c in range(chunk_count):
            write(c, result_buf[c] / rows_of(sum_buf[0], c))

    if lend:
        @pl.when(at_end)
        def _():
            for copy in lend_copies:
                copy.wait_send()
            shares = []
            for c in range(chunk_count):
                part_copy(c, 1).wait_recv()
                top, total = rows_of(top_buf[0], c), rows_of(sum_buf[0], c)
                stat = stat_buf[1, c]
                far_top = jnp.transpose(jnp.broadcast_to(stat[0:1], (LANES, chunk_rows)))
                far_total = jnp.transpose(jnp.broadcast_to(stat[1:2], (LANES, chunk_rows)))
                overall = jnp.maximum(top, far_top)
                factor, far_factor = jnp.exp2(top - overall), jnp.exp2(far_top - overall)
                inverse = 1.0 / (total * factor + far_total * far_factor)
                result_buf[c] = result_buf[c] * (factor * inverse)
                shares.append(far_factor * inverse)
            for c in range(chunk_count):
                part_copy(c, 0).wait_recv()
                write(c, result_buf[c] + part_buf[1, c].astype(jnp.float32) * shares[c])

        @pl.when(helper)
        def _():
            for i, ref in enumerate((part_buf, stat_buf)):
                send(ref.at[0], ref.at[1], part_send.at[i], part_send.at[i], {"blk": outward}).wait_send()


def shards(query_latent, query_rope, cache_latent, cache_rope, lengths, positions, value_weight):
    query_count, head_count, latent_width = query_latent.shape
    rope_width = query_rope.shape[1]
    token_count = cache_latent.shape[1]
    blk_count, sect_count, sub_count = (lax.axis_size(name) for name in ("blk", "sect", "sub"))
    own_heads, _, value_width = value_weight.shape
    chunk_heads = min(16, own_heads)
    chunk_count = own_heads // chunk_heads
    chunk_rows = query_count * chunk_heads
    block_rows = token_count + rope_width * token_count // latent_width
    rows = query_count * own_heads
    peers = max(sect_count - 1, 1)
    pairs = max(sub_count - 1, 1)
    bf16, f32 = jnp.bfloat16, jnp.float32
    hbm = pl.BlockSpec(memory_space=pltpu.HBM)
    vmem = pl.BlockSpec(memory_space=pltpu.VMEM)
    dma = pltpu.SemaphoreType.DMA
    return pl.pallas_call(
        functools.partial(kernel, (blk_count, sect_count, sub_count, chunk_heads)),
        out_shape=pltpu.VMEM((query_count, own_heads, value_width), bf16),
        in_specs=[hbm] * 7,
        out_specs=vmem,
        scratch_shapes=[
            pltpu.VMEM(query_rope.shape, bf16),
            pltpu.SMEM(lengths.shape, jnp.int32),
            pltpu.SMEM(positions.shape, jnp.int32),
            pltpu.VMEM((rope_width, token_count), bf16),
            pltpu.VMEM((2, query_count, own_heads, latent_width), bf16),
            pltpu.VMEM((query_count, head_count, rope_width), bf16),
            pltpu.VMEM((2, query_count, own_heads, rope_width), bf16),
            pltpu.VMEM((blk_count, sect_count, sub_count, block_rows, latent_width), bf16),
            pltpu.VMEM((own_heads, latent_width, value_width), bf16),
            pltpu.VMEM((2, query_count, LANES), jnp.int32),
            pltpu.VMEM((2, rows, LANES), jnp.int32),
            pltpu.VMEM((2, rows, LANES), f32),
            pltpu.VMEM((2, rows, LANES), f32),
            pltpu.VMEM((2, rows, latent_width), f32),
            pltpu.VMEM((chunk_count, chunk_rows, value_width), f32),
            pltpu.VMEM((2, chunk_count, chunk_rows, value_width), bf16),
            pltpu.VMEM((2, chunk_count, 8, chunk_rows), f32),
            dma((6,)),
            dma((2, max(blk_count - 1, 1))),
            dma((blk_count, PIECES)),
            dma((peers, blk_count)),
            dma((peers, blk_count, PIECES)),
            dma((pairs, blk_count)),
            dma((pairs, blk_count, sect_count)),
            dma((2,)),
            dma((2,)),
            dma((3,)),
            dma((3,)),
            dma((2,)),
            dma((chunk_count, 2)),
        ],
        compiler_params=pltpu.CompilerParams(
            collective_id=0, has_side_effects=True, vmem_limit_bytes=60 * 1024 * 1024
        ),
    )(query_latent, query_rope, cache_latent, cache_rope, lengths, positions, value_weight)


def solution(mesh):
    placed = (
        P(("rep", "blk"), None, None),
        P(("rep", "blk"), None, None),
        P(("rep", "blk", "sect", "sub"), None, None),
        P(("rep", "blk", "sect", "sub"), None, None),
        P("rep"),
        P(("rep", "blk")),
        P(("sect", "sub"), None, None),
    )
    return jax.shard_map(
        shards,
        mesh=mesh,
        in_specs=placed,
        out_specs=P(("rep", "blk"), ("sect", "sub"), None),
        check_vma=False,
    )
```

```python
import functools
import math

import jax
import jax.numpy as jnp
from jax import lax
from jax.experimental import pallas as pl
from jax.experimental.pallas import tpu as pltpu
from jax.sharding import PartitionSpec as P

lowest_score = -1e30
first_top = -1e29
LANES = 128
PIECES = 3
MESH = pl.DeviceIdType.MESH


def spread(column, width):
    return jnp.concatenate([column] * (width // LANES), axis=1)


def kernel(
    sizes, query_hbm, rope_q_hbm, latent_hbm, rope_hbm, length_hbm, position_hbm, weight_hbm,
    out_ref,
    rope_q_ref, length_ref, position_ref, rope_stage, query_buf, rope_q_buf, rope_rows_buf, cache_buf, weight_buf,
    mark_buf, place_buf, top_buf, sum_buf, acc_buf, result_buf, part_buf, stat_buf,
    local_sem, z_send, z_recv, x_send, x_recv, pair_send, pair_recv, side_send, side_recv,
    lend_send, lend_recv, part_send, part_recv,
):
    blk_count, sect_count, sub_count, chunk_heads = sizes
    _, query_count, own_heads, latent_width = query_buf.shape
    rope_width = rope_q_hbm.shape[1]
    token_count = latent_hbm.shape[1]
    value_width = weight_hbm.shape[2]
    folds = latent_width // token_count
    rope_rows_count = rope_width // folds
    block_rows = rope_rows_count + token_count
    bounds = [i * block_rows // PIECES for i in range(PIECES + 1)]
    rows = query_count * own_heads
    chunk_count = own_heads // chunk_heads
    chunk_rows = query_count * chunk_heads
    score_scale = math.log2(math.e) / math.sqrt(latent_width + rope_width)
    z = lax.axis_index("blk")
    x = lax.axis_index("sect")
    s = lax.axis_index("sub")
    last_z = blk_count - 1
    other = lax.rem(x + 1, sect_count)
    at_end = (z == 0) | (z == last_z)
    side = sect_count == 2
    lend = blk_count >= 4
    steps = last_z - 1 if lend else last_z
    helper = ((z == 1) | (z == last_z - 1)) if lend else (z < 0)

    barrier = pltpu.get_barrier_semaphore()

    def greet(device_id):
        pl.semaphore_signal(barrier, inc=1, device_id=device_id, device_id_type=MESH)

    for step in range(1, sub_count):
        greet({"sub": lax.rem(s + step, sub_count)})
    for step in range(1, sect_count):
        greet({"sect": lax.rem(x + step, sect_count)})

    @pl.when(z > 0)
    def _():
        greet({"blk": z - 1})

    @pl.when(z < last_z)
    def _():
        greet({"blk": z + 1})

    heads_at = pl.multiple_of((x * sub_count + s) * own_heads, own_heads)
    own_copies = [
        pltpu.make_async_copy(
            latent_hbm.at[0], cache_buf.at[z, x, s, pl.ds(rope_rows_count, token_count)], local_sem.at[0]
        ),
        pltpu.make_async_copy(rope_hbm.at[0], rope_stage, local_sem.at[1]),
    ]
    small_copies = [
        pltpu.make_async_copy(source, landing, local_sem.at[2 + i])
        for i, (source, landing) in enumerate((
            (rope_q_hbm, rope_q_ref), (length_hbm, length_ref), (position_hbm, position_ref),
            (query_hbm.at[:, pl.ds(heads_at, own_heads), :], query_buf.at[0]),
        ))
    ]
    weight_copy = pltpu.make_async_copy(weight_hbm, weight_buf, local_sem.at[0])
    for copy in own_copies + small_copies:
        copy.start()

    def send(source, landing, send_sem, recv_sem, device_id):
        return pltpu.make_async_remote_copy(
            src_ref=source, dst_ref=landing, send_sem=send_sem, recv_sem=recv_sem,
            device_id=device_id, device_id_type=MESH,
        )

    def place(j, xx, ss, first, end):
        return cache_buf.at[j, xx, ss, pl.ds(bounds[first], bounds[end] - bounds[first])]

    def block_send(j, xx, first, end, send_sem, recv_sem, device_id):
        here = place(j, xx, s, first, end)
        return send(here, here, send_sem, recv_sem, device_id)

    def await_block(j, xx, ss, first, end, recv_sem):
        here = place(j, xx, ss, first, end)
        send(here, here, recv_sem, recv_sem, {"sub": s}).wait_recv()

    def z_copy(j, p, way, target):
        away = z - j if way == 0 else j - z
        return block_send(j, x, p, p + 1, z_send.at[way, away], z_recv.at[j, p], {"blk": target})

    def x_copy(j, p, step):
        return block_send(
            j, x, p, p + 1, x_send.at[step - 1, j], x_recv.at[step - 1, j, p],
            {"sect": lax.rem(x + step, sect_count)},
        )

    def source_section(step):
        return lax.rem(x + sect_count - step, sect_count)

    def source_sub(step):
        return lax.rem(s + sub_count - step, sub_count)

    def to_pair(j, xx, first, end):
        for step in range(1, sub_count):
            block_send(
                j, xx, first, end, pair_send.at[step - 1, j], pair_recv.at[step - 1, j, xx],
                {"sub": lax.rem(s + step, sub_count)},
            ).start()

    def side_copy(j, way, target, first):
        return block_send(j, other, first, PIECES, side_send.at[way], side_recv.at[way], {"blk": target})

    inward = jnp.where(z == 0, 1, last_z - 1)
    outward = jnp.where(z == 1, 0, last_z)
    lend_copies = [
        send(ref.at[0], ref.at[1], lend_send.at[i], lend_recv.at[i], {"blk": inward})
        for i, ref in enumerate((query_buf, rope_rows_buf, mark_buf))
    ]

    def part_copy(c, i):
        ref = (part_buf, stat_buf)[i]
        return send(ref.at[0, c], ref.at[1, c], part_send.at[i], part_recv.at[c, i], {"blk": outward})

    neighbours = jnp.where(z > 0, 1, 0) + jnp.where(z < last_z, 1, 0)
    for copy in own_copies:
        copy.wait()
    for i in range(folds):
        cache_buf[z, x, s, 0:rope_rows_count, i * token_count:(i + 1) * token_count] = (
            rope_stage[i * rope_rows_count:(i + 1) * rope_rows_count, :]
        )
    pl.semaphore_wait(barrier, sub_count - 1 + sect_count - 1 + neighbours)

    for p in range(PIECES):
        @pl.when(z < last_z)
        def _():
            z_copy(z, p, 0, z + 1).start()

        @pl.when(z > 0)
        def _():
            z_copy(z, p, 1, z - 1).start()

        for step in range(1, sect_count):
            x_copy(z, p, step).start()
    to_pair(z, x, 0, PIECES)

    for copy in small_copies:
        copy.wait()
    for q in range(query_count):
        rope_q_buf[q] = jnp.transpose(rope_q_ref[q].astype(jnp.float32)).astype(jnp.bfloat16)
        mark_buf[0, q:q + 1, :] = jnp.full((1, LANES), position_ref[q], jnp.int32)
    rope_rows_buf[0] = rope_q_buf[:, pl.ds(heads_at, own_heads), :]
    if lend:
        @pl.when(at_end)
        def _():
            for copy in lend_copies:
                copy.start()
    weight_copy.start()

    def set_places(g):
        for q in range(query_count):
            place_buf[g, pl.ds(q * own_heads, own_heads), :] = jnp.broadcast_to(
                mark_buf[g, q:q + 1, :], (own_heads, LANES)
            )

    set_places(0)
    top_buf[...] = jnp.full(top_buf.shape, first_top, jnp.float32)
    sum_buf[...] = jnp.zeros(sum_buf.shape, jnp.float32)
    acc_buf[...] = jnp.zeros(acc_buf.shape, jnp.float32)

    def await_pair(j, xx):
        for step in range(1, sub_count):
            await_block(j, xx, source_sub(step), 0, PIECES, pair_recv.at[step - 1, j, xx])

    def absorb(entries, g):
        queries = query_buf[g].reshape(rows, latent_width)
        rope_rows = rope_rows_buf[g].reshape(rows, rope_width)
        offsets = lax.broadcasted_iota(jnp.int32, (rows, LANES), 1)
        parts = []
        for j, xx, valid in entries:
            for ss in range(sub_count):
                root = (j * sect_count + xx) * sub_count + ss
                block = cache_buf[j, xx, ss, rope_rows_count:block_rows, :]
                rope_block = jnp.concatenate([
                    cache_buf[j, xx, ss, 0:rope_rows_count, i * token_count:(i + 1) * token_count] for i in range(folds)
                ], axis=0)
                scores = lax.dot_general(
                    queries, block, (((1,), (1,)), ((), ())), preferred_element_type=jnp.float32,
                )
                scores = (scores + jnp.dot(rope_rows, rope_block, preferred_element_type=jnp.float32)) * score_scale
                length = length_ref[root]
                if valid is not None:
                    length = jnp.where(valid, length, 0)
                limit = jnp.minimum(length, place_buf[g] - (root * token_count - 1))
                for at in range(0, token_count, LANES):
                    parts.append(jnp.where(offsets < limit - at, scores[:, at:at + LANES], lowest_score))
        old_top = top_buf[g]
        best = functools.reduce(jnp.maximum, parts)
        new_top = jnp.maximum(old_top, jnp.max(best, axis=1, keepdims=True))
        factor = jnp.exp2(old_top - new_top)
        weights = [jnp.exp2(part - new_top) for part in parts]
        sum_buf[g] = sum_buf[g] * factor + jnp.sum(sum(weights), axis=1, keepdims=True)
        top_buf[g] = new_top
        mixed = acc_buf[g] * spread(factor, latent_width)
        per_entry = len(parts) // len(entries)
        for i, (j, xx, _) in enumerate(entries):
            block = cache_buf[j, xx, :, rope_rows_count:block_rows, :].reshape(sub_count * token_count, latent_width)
            mixed = mixed + jnp.dot(
                jnp.concatenate(
                    [part.astype(jnp.bfloat16) for part in weights[i * per_entry:(i + 1) * per_entry]], axis=1
                ),
                block, preferred_element_type=jnp.float32,
            )
        acc_buf[g] = mixed

    def inside(j):
        return (j >= 0) & (j < blk_count)

    def by_x(k, p):
        if not side or p == 0:
            return k == k
        return (k != 1) | at_end if p == 1 else k != 1

    def pass_on(k, p):
        for way in range(2):
            j = z - k if way == 0 else z + k
            target = z + 1 if way == 0 else z - 1

            @pl.when(inside(j))
            def _():
                await_block(j, x, s, p, p + 1, z_recv.at[j, p])

                @pl.when(inside(target) & ((k + 1 != last_z) if lend else (k == k)))
                def _():
                    z_copy(j, p, way, target).start()

                @pl.when(by_x(k, p))
                def _():
                    for step in range(1, sect_count):
                        x_copy(j, p, step).start()
                to_pair(j, x, p, p + 1)

    def take_sections(k, p):
        for way in range(2):
            j = z - k if way == 0 else z + k

            @pl.when(inside(j) & by_x(k, p) & ((k > 0) | (way == 0)))
            def _():
                for step in range(1, sect_count):
                    xx = source_section(step)
                    await_block(j, xx, s, p, p + 1, x_recv.at[step - 1, j, p])
                    to_pair(j, xx, p, p + 1)

    def sections(mine):
        return [x] if mine else [source_section(step) for step in range(1, sect_count)]

    def columns(k):
        return [z] if isinstance(k, int) and k == 0 else [z - k, z + k]

    def entries_at(k, mine, only=None):
        found = []
        for j in columns(k):
            valid = inside(j) if only is None else inside(j) & only
            for xx in sections(mine):
                here = jnp.where(valid, j, z)
                found.append((here, jnp.where(valid, xx, x), valid) if j is not z else (z, xx, None))
        return found

    def await_at(k, mine, only=None):
        for j in columns(k):
            @pl.when(inside(j) if only is None else inside(j) & only)
            def _():
                for xx in sections(mine):
                    await_pair(j, xx)

    def first_side(way_target):
        return (way_target == 0) | (way_target == last_z)

    def send_side():
        for way in range(2):
            target = z + 1 if way == 0 else z - 1
            for first in (1, 2):
                @pl.when(inside(target) & (first_side(target) == (first == 2)))
                def _():
                    side_copy(z, way, target, first).start()

    def take_side():
        for way in range(2):
            j = z - 1 if way == 0 else z + 1
            for first in (1, 2):
                @pl.when(inside(j) & (at_end == (first == 2)))
                def _():
                    await_block(j, other, s, first, PIECES, side_recv.at[way])
                    to_pair(j, other, first, PIECES)

    await_at(0, True)
    absorb(entries_at(0, True), 0)
    for p in range(PIECES):
        if steps > 0:
            pass_on(1, p)
        take_sections(0, p)
    if side and steps > 0:
        send_side()

    def one_step(k):
        behind = [] if side and isinstance(k, int) and k == 3 else [k - 2]
        only = (k != 3) if side and not isinstance(k, int) else None
        for p in range(PIECES):
            pass_on(k, p)
            if p == 0:
                await_at(k - 1, True)
                entries = entries_at(k - 1, True)
                for distance in behind:
                    await_at(distance, False, only)
                    entries = entries + entries_at(distance, False, only)
                absorb(entries, 0)
            else:
                take_sections(k - 1, p - 1)
        take_sections(k - 1, PIECES - 1)

    if steps <= 3:
        for k in range(2, steps + 1):
            one_step(k)
    else:
        one_step(2)

        def later_step(k, carry):
            one_step(k)
            return carry
        lax.fori_loop(3, steps + 1, later_step, 0)

    row_head = lax.rem(lax.broadcasted_iota(jnp.int32, (chunk_rows, value_width), 0), chunk_heads)

    def rows_of(value, c):
        width = value.shape[-1]
        part = value.reshape(query_count, own_heads, width)[:, c * chunk_heads:(c + 1) * chunk_heads, :]
        return part.reshape(chunk_rows, width)

    def project(g, c):
        latent = rows_of(acc_buf[g], c).astype(jnp.bfloat16)
        result = jnp.zeros((chunk_rows, value_width), jnp.float32)
        for h in range(0, chunk_heads, 2):
            pair = jnp.concatenate(
                [weight_buf[c * chunk_heads + h], weight_buf[c * chunk_heads + h + 1]], axis=1
            )
            both = jnp.dot(latent, pair, preferred_element_type=jnp.float32)
            result = jnp.where(row_head == h, both[:, :value_width], result)
            result = jnp.where(row_head == h + 1, both[:, value_width:], result)
        return result

    def take_lent():
        for copy in lend_copies:
            copy.wait_recv()
        set_places(1)
        absorb(far_mine, 0)
        absorb(far_mine, 1)

    def return_parts():
        absorb(far_others, 1)
        for c in range(chunk_count):
            tops, totals = (jnp.transpose(rows_of(ref[1], c))[0:8] for ref in (top_buf, sum_buf))
            stat_buf[0, c] = jnp.where(lax.broadcasted_iota(jnp.int32, tops.shape, 0) == 0, tops, totals)
            part_copy(c, 1).start()
        for c in range(chunk_count):
            part_buf[0, c] = project(1, c).astype(jnp.bfloat16)
            part_copy(c, 0).start()

    if steps == 0:
        await_at(0, False)
        if sect_count > 1:
            absorb(entries_at(0, False), 0)
    else:
        far = jnp.where(z >= steps, z - steps, z + steps)
        has_far = inside(far)
        far = jnp.where(has_far, far, z)
        far_mine = [(far, x, has_far)]
        far_others = [(far, jnp.where(has_far, xx, x), has_far) for xx in sections(False)]
        await_at(steps, True)
        if lend:
            pl.when(helper)(take_lent)

            @pl.when(jnp.logical_not(helper))
            def _():
                absorb(far_mine, 0)
        else:
            absorb(far_mine, 0)
        for p in range(PIECES):
            take_sections(steps, p)
        if side:
            take_side()
        weight_copy.wait()
        await_at(steps, False)
        if lend:
            pl.when(helper)(return_parts)
        left = sorted({steps - 1} | ({1} if side and steps > 1 else set()))
        rest = list(far_others)
        for k in left:
            await_at(k, False)
            rest = rest + entries_at(k, False)
        if rest and lend and side and steps == 2:
            @pl.when(at_end)
            def _():
                near = jnp.where(z == 0, 1, last_z - 1)
                absorb(far_others + [(near, other, None)], 0)

            @pl.when(jnp.logical_not(at_end))
            def _():
                absorb(rest, 0)
        elif rest:
            absorb(rest, 0)

    def drain(j, carry):
        def whole_wait(xx, sem):
            block_send(j, xx, 0, PIECES, sem, sem, {"sub": s}).wait_send()

        far_up = ((j == 0) & (z + 1 == last_z)) if lend else (j < 0)
        far_down = ((j == last_z) & (z == 1)) if lend else (j < 0)
        here = ((j - z != last_z) & (z - j != last_z)) if lend else (j >= 0)

        @pl.when((j <= z) & (z < last_z) & jnp.logical_not(far_up))
        def _():
            whole_wait(x, z_send.at[0, z - j])

        @pl.when((j >= z) & (z > 0) & jnp.logical_not(far_down))
        def _():
            whole_wait(x, z_send.at[1, j - z])

        near = ((j == z - 1) | (j == z + 1)) if side else (j < 0)
        for step in range(1, sect_count):
            sem = x_send.at[step - 1, j]
            for end in (1, 2):
                @pl.when(near & (at_end == (end == 2)))
                def _():
                    block_send(j, x, 0, end, sem, sem, {"sub": s}).wait_send()

            @pl.when(here & jnp.logical_not(near))
            def _():
                whole_wait(x, sem)

        @pl.when(here)
        def _():
            for step in range(1, sub_count):
                all_sections, sem = cache_buf.at[j, :, s], pair_send.at[step - 1, j]
                send(all_sections, all_sections, sem, sem, {"sub": s}).wait_send()
        return carry

    lax.fori_loop(0, blk_count, drain, 0)
    if side:
        for way in range(2):
            target = z + 1 if way == 0 else z - 1
            for first in (1, 2):
                @pl.when(inside(target) & (first_side(target) == (first == 2)))
                def _():
                    side_copy(z, way, z, first).wait_send()

    for c in range(chunk_count):
        result_buf[c] = project(0, c)

    def write(c, value):
        out_ref[:, c * chunk_heads:(c + 1) * chunk_heads, :] = value.reshape(
            query_count, chunk_heads, value_width
        ).astype(out_ref.dtype)

    merged = at_end if lend else (z < 0)

    @pl.when(jnp.logical_not(merged))
    def _():
        for c in range(chunk_count):
            write(c, result_buf[c] / rows_of(sum_buf[0], c))

    if lend:
        @pl.when(at_end)
        def _():
            for copy in lend_copies:
                copy.wait_send()
            shares = []
            for c in range(chunk_count):
                part_copy(c, 1).wait_recv()
                top, total = rows_of(top_buf[0], c), rows_of(sum_buf[0], c)
                stat = stat_buf[1, c]
                far_top = jnp.transpose(jnp.broadcast_to(stat[0:1], (LANES, chunk_rows)))
                far_total = jnp.transpose(jnp.broadcast_to(stat[1:2], (LANES, chunk_rows)))
                overall = jnp.maximum(top, far_top)
                factor, far_factor = jnp.exp2(top - overall), jnp.exp2(far_top - overall)
                inverse = 1.0 / (total * factor + far_total * far_factor)
                result_buf[c] = result_buf[c] * (factor * inverse)
                shares.append(far_factor * inverse)
            for c in range(chunk_count):
                part_copy(c, 0).wait_recv()
                write(c, result_buf[c] + part_buf[1, c].astype(jnp.float32) * shares[c])

        @pl.when(helper)
        def _():
            for i, ref in enumerate((part_buf, stat_buf)):
                send(ref.at[0], ref.at[1], part_send.at[i], part_send.at[i], {"blk": outward}).wait_send()


def shards(query_latent, query_rope, cache_latent, cache_rope, lengths, positions, value_weight):
    query_count, head_count, latent_width = query_latent.shape
    rope_width = query_rope.shape[1]
    token_count = cache_latent.shape[1]
    blk_count, sect_count, sub_count = (lax.axis_size(name) for name in ("blk", "sect", "sub"))
    own_heads, _, value_width = value_weight.shape
    chunk_heads = min(16, own_heads)
    chunk_count = own_heads // chunk_heads
    chunk_rows = query_count * chunk_heads
    block_rows = token_count + rope_width * token_count // latent_width
    rows = query_count * own_heads
    peers = max(sect_count - 1, 1)
    pairs = max(sub_count - 1, 1)
    bf16, f32 = jnp.bfloat16, jnp.float32
    hbm = pl.BlockSpec(memory_space=pltpu.HBM)
    vmem = pl.BlockSpec(memory_space=pltpu.VMEM)
    dma = pltpu.SemaphoreType.DMA
    return pl.pallas_call(
        functools.partial(kernel, (blk_count, sect_count, sub_count, chunk_heads)),
        out_shape=pltpu.VMEM((query_count, own_heads, value_width), bf16),
        in_specs=[hbm] * 7,
        out_specs=vmem,
        scratch_shapes=[
            pltpu.VMEM(query_rope.shape, bf16),
            pltpu.SMEM(lengths.shape, jnp.int32),
            pltpu.SMEM(positions.shape, jnp.int32),
            pltpu.VMEM((rope_width, token_count), bf16),
            pltpu.VMEM((2, query_count, own_heads, latent_width), bf16),
            pltpu.VMEM((query_count, head_count, rope_width), bf16),
            pltpu.VMEM((2, query_count, own_heads, rope_width), bf16),
            pltpu.VMEM((blk_count, sect_count, sub_count, block_rows, latent_width), bf16),
            pltpu.VMEM((own_heads, latent_width, value_width), bf16),
            pltpu.VMEM((2, query_count, LANES), jnp.int32),
            pltpu.VMEM((2, rows, LANES), jnp.int32),
            pltpu.VMEM((2, rows, LANES), f32),
            pltpu.VMEM((2, rows, LANES), f32),
            pltpu.VMEM((2, rows, latent_width), f32),
            pltpu.VMEM((chunk_count, chunk_rows, value_width), f32),
            pltpu.VMEM((2, chunk_count, chunk_rows, value_width), bf16),
            pltpu.VMEM((2, chunk_count, 8, chunk_rows), f32),
            dma((6,)),
            dma((2, max(blk_count - 2 if blk_count >= 4 else blk_count - 1, 1))),
            dma((blk_count, PIECES)),
            dma((peers, blk_count)),
            dma((peers, blk_count, PIECES)),
            dma((pairs, blk_count)),
            dma((pairs, blk_count, sect_count)),
            dma((2,)),
            dma((2,)),
            dma((3,)),
            dma((3,)),
            dma((2,)),
            dma((chunk_count, 2)),
        ],
        compiler_params=pltpu.CompilerParams(
            collective_id=0, has_side_effects=True, vmem_limit_bytes=60 * 1024 * 1024
        ),
    )(query_latent, query_rope, cache_latent, cache_rope, lengths, positions, value_weight)


def solution(mesh):
    placed = (
        P(("rep", "blk"), None, None),
        P(("rep", "blk"), None, None),
        P(("rep", "blk", "sect", "sub"), None, None),
        P(("rep", "blk", "sect", "sub"), None, None),
        P("rep"),
        P(("rep", "blk")),
        P(("sect", "sub"), None, None),
    )
    return jax.shard_map(
        shards,
        mesh=mesh,
        in_specs=placed,
        out_specs=P(("rep", "blk"), ("sect", "sub"), None),
        check_vma=False,
    )
```

```python
import functools
import math

import jax
import jax.numpy as jnp
from jax import lax
from jax.experimental import pallas as pl
from jax.experimental.pallas import tpu as pltpu
from jax.sharding import PartitionSpec as P

lowest_score = -1e30
first_top = -1e29
LANES = 128
PIECES = 3
MESH = pl.DeviceIdType.MESH


def spread(column, width):
    return jnp.concatenate([column] * (width // LANES), axis=1)


def kernel(
    sizes, query_hbm, rope_q_hbm, latent_hbm, rope_hbm, length_hbm, position_hbm, weight_hbm,
    out_ref,
    rope_q_ref, length_ref, position_ref, rope_stage, query_buf, rope_q_buf, rope_rows_buf, cache_buf, weight_buf,
    mark_buf, place_buf, top_buf, sum_buf, acc_buf, result_buf, part_buf, stat_buf,
    local_sem, z_send, z_recv, x_send, x_recv, pair_send, pair_recv, side_send, side_recv,
    lend_send, lend_recv, part_send, part_recv,
):
    blk_count, sect_count, sub_count, chunk_heads = sizes
    _, query_count, own_heads, latent_width = query_buf.shape
    rope_width = rope_q_hbm.shape[1]
    token_count = latent_hbm.shape[1]
    value_width = weight_hbm.shape[2]
    folds = latent_width // token_count
    rope_rows_count = rope_width // folds
    block_rows = rope_rows_count + token_count
    bounds = [i * block_rows // PIECES for i in range(PIECES + 1)]
    bounds[1] -= 16
    rows = query_count * own_heads
    chunk_count = own_heads // chunk_heads
    chunk_rows = query_count * chunk_heads
    score_scale = math.log2(math.e) / math.sqrt(latent_width + rope_width)
    z = lax.axis_index("blk")
    x = lax.axis_index("sect")
    s = lax.axis_index("sub")
    last_z = blk_count - 1
    other = lax.rem(x + 1, sect_count)
    at_end = (z == 0) | (z == last_z)
    side = sect_count == 2
    lend = blk_count >= 4
    steps = last_z - 1 if lend else last_z
    helper = ((z == 1) | (z == last_z - 1)) if lend else (z < 0)

    barrier = pltpu.get_barrier_semaphore()

    def greet(device_id):
        pl.semaphore_signal(barrier, inc=1, device_id=device_id, device_id_type=MESH)

    for step in range(1, sub_count):
        greet({"sub": lax.rem(s + step, sub_count)})
    for step in range(1, sect_count):
        greet({"sect": lax.rem(x + step, sect_count)})

    @pl.when(z > 0)
    def _():
        greet({"blk": z - 1})

    @pl.when(z < last_z)
    def _():
        greet({"blk": z + 1})

    heads_at = pl.multiple_of((x * sub_count + s) * own_heads, own_heads)
    own_copies = [
        pltpu.make_async_copy(
            latent_hbm.at[0], cache_buf.at[z, x, s, pl.ds(rope_rows_count, token_count)], local_sem.at[0]
        ),
        pltpu.make_async_copy(rope_hbm.at[0], rope_stage, local_sem.at[1]),
    ]
    small_copies = [
        pltpu.make_async_copy(source, landing, local_sem.at[2 + i])
        for i, (source, landing) in enumerate((
            (rope_q_hbm, rope_q_ref), (length_hbm, length_ref), (position_hbm, position_ref),
            (query_hbm.at[:, pl.ds(heads_at, own_heads), :], query_buf.at[0]),
        ))
    ]
    weight_copy = pltpu.make_async_copy(weight_hbm, weight_buf, local_sem.at[0])
    for copy in own_copies + small_copies:
        copy.start()

    def send(source, landing, send_sem, recv_sem, device_id):
        return pltpu.make_async_remote_copy(
            src_ref=source, dst_ref=landing, send_sem=send_sem, recv_sem=recv_sem,
            device_id=device_id, device_id_type=MESH,
        )

    def place(j, xx, ss, first, end):
        return cache_buf.at[j, xx, ss, pl.ds(bounds[first], bounds[end] - bounds[first])]

    def block_send(j, xx, first, end, send_sem, recv_sem, device_id):
        here = place(j, xx, s, first, end)
        return send(here, here, send_sem, recv_sem, device_id)

    def await_block(j, xx, ss, first, end, recv_sem):
        here = place(j, xx, ss, first, end)
        send(here, here, recv_sem, recv_sem, {"sub": s}).wait_recv()

    def z_copy(j, p, way, target):
        away = z - j if way == 0 else j - z
        return block_send(j, x, p, p + 1, z_send.at[way, away], z_recv.at[j, p], {"blk": target})

    def x_copy(j, p, step):
        return block_send(
            j, x, p, p + 1, x_send.at[step - 1, j], x_recv.at[step - 1, j, p],
            {"sect": lax.rem(x + step, sect_count)},
        )

    def source_section(step):
        return lax.rem(x + sect_count - step, sect_count)

    def source_sub(step):
        return lax.rem(s + sub_count - step, sub_count)

    def to_pair(j, xx, first, end):
        for step in range(1, sub_count):
            block_send(
                j, xx, first, end, pair_send.at[step - 1, j], pair_recv.at[step - 1, j, xx],
                {"sub": lax.rem(s + step, sub_count)},
            ).start()

    def side_copy(j, way, target, first):
        return block_send(j, other, first, PIECES, side_send.at[way], side_recv.at[way], {"blk": target})

    inward = jnp.where(z == 0, 1, last_z - 1)
    outward = jnp.where(z == 1, 0, last_z)
    lend_copies = [
        send(ref.at[0], ref.at[1], lend_send.at[i], lend_recv.at[i], {"blk": inward})
        for i, ref in enumerate((query_buf, rope_rows_buf, mark_buf))
    ]

    def part_copy(c, i):
        ref = (part_buf, stat_buf)[i]
        return send(ref.at[0, c], ref.at[1, c], part_send.at[i], part_recv.at[c, i], {"blk": outward})

    neighbours = jnp.where(z > 0, 1, 0) + jnp.where(z < last_z, 1, 0)
    for copy in own_copies:
        copy.wait()
    for i in range(folds):
        cache_buf[z, x, s, 0:rope_rows_count, i * token_count:(i + 1) * token_count] = (
            rope_stage[i * rope_rows_count:(i + 1) * rope_rows_count, :]
        )
    pl.semaphore_wait(barrier, sub_count - 1 + sect_count - 1 + neighbours)

    for p in range(PIECES):
        @pl.when(z < last_z)
        def _():
            z_copy(z, p, 0, z + 1).start()

        @pl.when(z > 0)
        def _():
            z_copy(z, p, 1, z - 1).start()

        for step in range(1, sect_count):
            x_copy(z, p, step).start()
    to_pair(z, x, 0, PIECES)

    for copy in small_copies:
        copy.wait()
    for q in range(query_count):
        rope_q_buf[q] = jnp.transpose(rope_q_ref[q].astype(jnp.float32)).astype(jnp.bfloat16)
        mark_buf[0, q:q + 1, :] = jnp.full((1, LANES), position_ref[q], jnp.int32)
    rope_rows_buf[0] = rope_q_buf[:, pl.ds(heads_at, own_heads), :]
    if lend:
        @pl.when(at_end)
        def _():
            for copy in lend_copies:
                copy.start()
    weight_copy.start()

    def set_places(g):
        for q in range(query_count):
            place_buf[g, pl.ds(q * own_heads, own_heads), :] = jnp.broadcast_to(
                mark_buf[g, q:q + 1, :], (own_heads, LANES)
            )

    set_places(0)
    top_buf[...] = jnp.full(top_buf.shape, first_top, jnp.float32)
    sum_buf[...] = jnp.zeros(sum_buf.shape, jnp.float32)
    acc_buf[...] = jnp.zeros(acc_buf.shape, jnp.float32)

    def await_pair(j, xx):
        for step in range(1, sub_count):
            await_block(j, xx, source_sub(step), 0, PIECES, pair_recv.at[step - 1, j, xx])

    def absorb(entries, g):
        queries = query_buf[g].reshape(rows, latent_width)
        rope_rows = rope_rows_buf[g].reshape(rows, rope_width)
        offsets = lax.broadcasted_iota(jnp.int32, (rows, LANES), 1)
        parts = []
        for j, xx, valid in entries:
            for ss in range(sub_count):
                root = (j * sect_count + xx) * sub_count + ss
                block = cache_buf[j, xx, ss, rope_rows_count:block_rows, :]
                rope_block = jnp.concatenate([
                    cache_buf[j, xx, ss, 0:rope_rows_count, i * token_count:(i + 1) * token_count] for i in range(folds)
                ], axis=0)
                scores = lax.dot_general(
                    queries, block, (((1,), (1,)), ((), ())), preferred_element_type=jnp.float32,
                )
                scores = (scores + jnp.dot(rope_rows, rope_block, preferred_element_type=jnp.float32)) * score_scale
                length = length_ref[root]
                if valid is not None:
                    length = jnp.where(valid, length, 0)
                limit = jnp.minimum(length, place_buf[g] - (root * token_count - 1))
                for at in range(0, token_count, LANES):
                    parts.append(jnp.where(offsets < limit - at, scores[:, at:at + LANES], lowest_score))
        old_top = top_buf[g]
        best = functools.reduce(jnp.maximum, parts)
        new_top = jnp.maximum(old_top, jnp.max(best, axis=1, keepdims=True))
        factor = jnp.exp2(old_top - new_top)
        weights = [jnp.exp2(part - new_top) for part in parts]
        sum_buf[g] = sum_buf[g] * factor + jnp.sum(sum(weights), axis=1, keepdims=True)
        top_buf[g] = new_top
        mixed = acc_buf[g] * spread(factor, latent_width)
        per_entry = len(parts) // len(entries)
        for i, (j, xx, _) in enumerate(entries):
            block = cache_buf[j, xx, :, rope_rows_count:block_rows, :].reshape(sub_count * token_count, latent_width)
            mixed = mixed + jnp.dot(
                jnp.concatenate(
                    [part.astype(jnp.bfloat16) for part in weights[i * per_entry:(i + 1) * per_entry]], axis=1
                ),
                block, preferred_element_type=jnp.float32,
            )
        acc_buf[g] = mixed

    def inside(j):
        return (j >= 0) & (j < blk_count)

    def by_x(k, p):
        if not side or p == 0:
            return k == k
        return (k != 1) | at_end if p == 1 else k != 1

    def pass_on(k, p):
        for way in range(2):
            j = z - k if way == 0 else z + k
            target = z + 1 if way == 0 else z - 1

            @pl.when(inside(j))
            def _():
                await_block(j, x, s, p, p + 1, z_recv.at[j, p])

                @pl.when(inside(target) & ((k + 1 != last_z) if lend else (k == k)))
                def _():
                    z_copy(j, p, way, target).start()

                @pl.when(by_x(k, p))
                def _():
                    for step in range(1, sect_count):
                        x_copy(j, p, step).start()
                to_pair(j, x, p, p + 1)

    def take_sections(k, p):
        for way in range(2):
            j = z - k if way == 0 else z + k

            @pl.when(inside(j) & by_x(k, p) & ((k > 0) | (way == 0)))
            def _():
                for step in range(1, sect_count):
                    xx = source_section(step)
                    await_block(j, xx, s, p, p + 1, x_recv.at[step - 1, j, p])
                    to_pair(j, xx, p, p + 1)

    def sections(mine):
        return [x] if mine else [source_section(step) for step in range(1, sect_count)]

    def columns(k):
        return [z] if isinstance(k, int) and k == 0 else [z - k, z + k]

    def entries_at(k, mine, only=None):
        found = []
        for j in columns(k):
            valid = inside(j) if only is None else inside(j) & only
            for xx in sections(mine):
                here = jnp.where(valid, j, z)
                found.append((here, jnp.where(valid, xx, x), valid) if j is not z else (z, xx, None))
        return found

    def await_at(k, mine, only=None):
        for j in columns(k):
            @pl.when(inside(j) if only is None else inside(j) & only)
            def _():
                for xx in sections(mine):
                    await_pair(j, xx)

    def first_side(way_target):
        return (way_target == 0) | (way_target == last_z)

    def send_side():
        for way in range(2):
            target = z + 1 if way == 0 else z - 1
            for first in (1, 2):
                @pl.when(inside(target) & (first_side(target) == (first == 2)))
                def _():
                    side_copy(z, way, target, first).start()

    def take_side():
        for way in range(2):
            j = z - 1 if way == 0 else z + 1
            for first in (1, 2):
                @pl.when(inside(j) & (at_end == (first == 2)))
                def _():
                    await_block(j, other, s, first, PIECES, side_recv.at[way])
                    to_pair(j, other, first, PIECES)

    await_at(0, True)
    absorb(entries_at(0, True), 0)
    for p in range(PIECES):
        if steps > 0:
            pass_on(1, p)
        take_sections(0, p)
    if side and steps > 0:
        send_side()

    def one_step(k):
        behind = [] if side and isinstance(k, int) and k == 3 else [k - 2]
        only = (k != 3) if side and not isinstance(k, int) else None
        for p in range(PIECES):
            pass_on(k, p)
            if p == 0:
                await_at(k - 1, True)
                entries = entries_at(k - 1, True)
                for distance in behind:
                    await_at(distance, False, only)
                    entries = entries + entries_at(distance, False, only)
                absorb(entries, 0)
            else:
                take_sections(k - 1, p - 1)
        take_sections(k - 1, PIECES - 1)

    if steps <= 3:
        for k in range(2, steps + 1):
            one_step(k)
    else:
        one_step(2)

        def later_step(k, carry):
            one_step(k)
            return carry
        lax.fori_loop(3, steps + 1, later_step, 0)

    row_head = lax.rem(lax.broadcasted_iota(jnp.int32, (chunk_rows, value_width), 0), chunk_heads)

    def rows_of(value, c):
        width = value.shape[-1]
        part = value.reshape(query_count, own_heads, width)[:, c * chunk_heads:(c + 1) * chunk_heads, :]
        return part.reshape(chunk_rows, width)

    def project(g, c):
        latent = rows_of(acc_buf[g], c).astype(jnp.bfloat16)
        result = jnp.zeros((chunk_rows, value_width), jnp.float32)
        for h in range(0, chunk_heads, 2):
            pair = jnp.concatenate(
                [weight_buf[c * chunk_heads + h], weight_buf[c * chunk_heads + h + 1]], axis=1
            )
            both = jnp.dot(latent, pair, preferred_element_type=jnp.float32)
            result = jnp.where(row_head == h, both[:, :value_width], result)
            result = jnp.where(row_head == h + 1, both[:, value_width:], result)
        return result

    def take_lent():
        for copy in lend_copies:
            copy.wait_recv()
        set_places(1)
        absorb(far_mine, 0)
        absorb(far_mine, 1)

    def return_parts():
        absorb(far_others, 1)
        for c in range(chunk_count):
            tops, totals = (jnp.transpose(rows_of(ref[1], c))[0:8] for ref in (top_buf, sum_buf))
            stat_buf[0, c] = jnp.where(lax.broadcasted_iota(jnp.int32, tops.shape, 0) == 0, tops, totals)
            part_copy(c, 1).start()
        for c in range(chunk_count):
            part_buf[0, c] = project(1, c).astype(jnp.bfloat16)
            part_copy(c, 0).start()

    if steps == 0:
        await_at(0, False)
        if sect_count > 1:
            absorb(entries_at(0, False), 0)
    else:
        far = jnp.where(z >= steps, z - steps, z + steps)
        has_far = inside(far)
        far = jnp.where(has_far, far, z)
        far_mine = [(far, x, has_far)]
        far_others = [(far, jnp.where(has_far, xx, x), has_far) for xx in sections(False)]
        await_at(steps, True)
        if lend:
            pl.when(helper)(take_lent)

            @pl.when(jnp.logical_not(helper))
            def _():
                absorb(far_mine, 0)
        else:
            absorb(far_mine, 0)
        for p in range(PIECES):
            take_sections(steps, p)
        if side:
            take_side()
        weight_copy.wait()
        await_at(steps, False)
        if lend:
            pl.when(helper)(return_parts)
        left = sorted({steps - 1} | ({1} if side and steps > 1 else set()))
        rest = list(far_others)
        for k in left:
            await_at(k, False)
            rest = rest + entries_at(k, False)
        if rest and lend and side and steps == 2:
            @pl.when(at_end)
            def _():
                near = jnp.where(z == 0, 1, last_z - 1)
                absorb(far_others + [(near, other, None)], 0)

            @pl.when(jnp.logical_not(at_end))
            def _():
                absorb(rest, 0)
        elif rest:
            absorb(rest, 0)

    def drain(j, carry):
        def whole_wait(xx, sem):
            block_send(j, xx, 0, PIECES, sem, sem, {"sub": s}).wait_send()

        far_up = ((j == 0) & (z + 1 == last_z)) if lend else (j < 0)
        far_down = ((j == last_z) & (z == 1)) if lend else (j < 0)
        here = ((j - z != last_z) & (z - j != last_z)) if lend else (j >= 0)

        @pl.when((j <= z) & (z < last_z) & jnp.logical_not(far_up))
        def _():
            whole_wait(x, z_send.at[0, z - j])

        @pl.when((j >= z) & (z > 0) & jnp.logical_not(far_down))
        def _():
            whole_wait(x, z_send.at[1, j - z])

        near = ((j == z - 1) | (j == z + 1)) if side else (j < 0)
        for step in range(1, sect_count):
            sem = x_send.at[step - 1, j]
            for end in (1, 2):
                @pl.when(near & (at_end == (end == 2)))
                def _():
                    block_send(j, x, 0, end, sem, sem, {"sub": s}).wait_send()

            @pl.when(here & jnp.logical_not(near))
            def _():
                whole_wait(x, sem)

        @pl.when(here)
        def _():
            for step in range(1, sub_count):
                all_sections, sem = cache_buf.at[j, :, s], pair_send.at[step - 1, j]
                send(all_sections, all_sections, sem, sem, {"sub": s}).wait_send()
        return carry

    lax.fori_loop(0, blk_count, drain, 0)
    if side:
        for way in range(2):
            target = z + 1 if way == 0 else z - 1
            for first in (1, 2):
                @pl.when(inside(target) & (first_side(target) == (first == 2)))
                def _():
                    side_copy(z, way, z, first).wait_send()

    for c in range(chunk_count):
        result_buf[c] = project(0, c)

    def write(c, value):
        out_ref[:, c * chunk_heads:(c + 1) * chunk_heads, :] = value.reshape(
            query_count, chunk_heads, value_width
        ).astype(out_ref.dtype)

    merged = at_end if lend else (z < 0)

    @pl.when(jnp.logical_not(merged))
    def _():
        for c in range(chunk_count):
            write(c, result_buf[c] / rows_of(sum_buf[0], c))

    if lend:
        @pl.when(at_end)
        def _():
            for copy in lend_copies:
                copy.wait_send()
            shares = []
            for c in range(chunk_count):
                part_copy(c, 1).wait_recv()
                top, total = rows_of(top_buf[0], c), rows_of(sum_buf[0], c)
                stat = stat_buf[1, c]
                far_top = jnp.transpose(jnp.broadcast_to(stat[0:1], (LANES, chunk_rows)))
                far_total = jnp.transpose(jnp.broadcast_to(stat[1:2], (LANES, chunk_rows)))
                overall = jnp.maximum(top, far_top)
                factor, far_factor = jnp.exp2(top - overall), jnp.exp2(far_top - overall)
                inverse = 1.0 / (total * factor + far_total * far_factor)
                result_buf[c] = result_buf[c] * (factor * inverse)
                shares.append(far_factor * inverse)
            for c in range(chunk_count):
                part_copy(c, 0).wait_recv()
                write(c, result_buf[c] + part_buf[1, c].astype(jnp.float32) * shares[c])

        @pl.when(helper)
        def _():
            for i, ref in enumerate((part_buf, stat_buf)):
                send(ref.at[0], ref.at[1], part_send.at[i], part_send.at[i], {"blk": outward}).wait_send()


def shards(query_latent, query_rope, cache_latent, cache_rope, lengths, positions, value_weight):
    query_count, head_count, latent_width = query_latent.shape
    rope_width = query_rope.shape[1]
    token_count = cache_latent.shape[1]
    blk_count, sect_count, sub_count = (lax.axis_size(name) for name in ("blk", "sect", "sub"))
    own_heads, _, value_width = value_weight.shape
    chunk_heads = min(16, own_heads)
    chunk_count = own_heads // chunk_heads
    chunk_rows = query_count * chunk_heads
    block_rows = token_count + rope_width * token_count // latent_width
    rows = query_count * own_heads
    peers = max(sect_count - 1, 1)
    pairs = max(sub_count - 1, 1)
    bf16, f32 = jnp.bfloat16, jnp.float32
    hbm = pl.BlockSpec(memory_space=pltpu.HBM)
    vmem = pl.BlockSpec(memory_space=pltpu.VMEM)
    dma = pltpu.SemaphoreType.DMA
    return pl.pallas_call(
        functools.partial(kernel, (blk_count, sect_count, sub_count, chunk_heads)),
        out_shape=pltpu.VMEM((query_count, own_heads, value_width), bf16),
        in_specs=[hbm] * 7,
        out_specs=vmem,
        scratch_shapes=[
            pltpu.VMEM(query_rope.shape, bf16),
            pltpu.SMEM(lengths.shape, jnp.int32),
            pltpu.SMEM(positions.shape, jnp.int32),
            pltpu.VMEM((rope_width, token_count), bf16),
            pltpu.VMEM((2, query_count, own_heads, latent_width), bf16),
            pltpu.VMEM((query_count, head_count, rope_width), bf16),
            pltpu.VMEM((2, query_count, own_heads, rope_width), bf16),
            pltpu.VMEM((blk_count, sect_count, sub_count, block_rows, latent_width), bf16),
            pltpu.VMEM((own_heads, latent_width, value_width), bf16),
            pltpu.VMEM((2, query_count, LANES), jnp.int32),
            pltpu.VMEM((2, rows, LANES), jnp.int32),
            pltpu.VMEM((2, rows, LANES), f32),
            pltpu.VMEM((2, rows, LANES), f32),
            pltpu.VMEM((2, rows, latent_width), f32),
            pltpu.VMEM((chunk_count, chunk_rows, value_width), f32),
            pltpu.VMEM((2, chunk_count, chunk_rows, value_width), bf16),
            pltpu.VMEM((2, chunk_count, 8, chunk_rows), f32),
            dma((6,)),
            dma((2, max(blk_count - 2 if blk_count >= 4 else blk_count - 1, 1))),
            dma((blk_count, PIECES)),
            dma((peers, blk_count)),
            dma((peers, blk_count, PIECES)),
            dma((pairs, blk_count)),
            dma((pairs, blk_count, sect_count)),
            dma((2,)),
            dma((2,)),
            dma((3,)),
            dma((3,)),
            dma((2,)),
            dma((chunk_count, 2)),
        ],
        compiler_params=pltpu.CompilerParams(
            collective_id=0, has_side_effects=True, vmem_limit_bytes=60 * 1024 * 1024
        ),
    )(query_latent, query_rope, cache_latent, cache_rope, lengths, positions, value_weight)


def solution(mesh):
    placed = (
        P(("rep", "blk"), None, None),
        P(("rep", "blk"), None, None),
        P(("rep", "blk", "sect", "sub"), None, None),
        P(("rep", "blk", "sect", "sub"), None, None),
        P("rep"),
        P(("rep", "blk")),
        P(("sect", "sub"), None, None),
    )
    return jax.shard_map(
        shards,
        mesh=mesh,
        in_specs=placed,
        out_specs=P(("rep", "blk"), ("sect", "sub"), None),
        check_vma=False,
    )
```
